256 devices in a mesh: head: 8 (over y, x_lo), seq: 32 (over z, x_hi, core).
Axes of the slice: x: 4 (x_hi: 2, x_lo: 2; x = x_hi * 2 + x_lo), y: 4, z: 8, core: 2. Of those that a mesh axis runs over, the one named last changes fastest.
Arguments:
- query: bfloat16 [32768, 3072], P(('seq', 'head')), may hold values from -9 to 9
- key: bfloat16 [32768, 3072], P(('seq', 'head')), may hold values from -9 to 9
- value: bfloat16 [32768, 3072], P(('seq', 'head')), may hold values from -6 to 6
- grad_out: bfloat16 [32768, 3072], P(('seq', 'head')), may hold values from -6 to 6
- tile_list: int32 [256, 12], replicated, may hold values from 0 to 255, as said below
- tile_count: int32 [256], replicated, may hold values from 1 to 12, as said below
Outputs:
- attn_out: bfloat16 [32768, 3072], P(('seq', 'head'))
- grad_query: bfloat16 [32768, 3072], P(('seq', 'head'))
- grad_key: bfloat16 [32768, 3072], P(('seq', 'head'))
- grad_value: bfloat16 [32768, 3072], P(('seq', 'head'))
The draws below stay inside these ranges and needn't reach their ends.
Inputs may be any that keep to these rules, and one draw needn't show every extreme that they name: `tile_list`: tile g sits at frame block g // 8, tile row (g // 2) % 4 and tile column g % 2. Row a lists only tiles at most one step from tile a along each of the three tile axes; its first entry is a itself; its first tile_count[a] entries are distinct; entries from tile_count[a] on are to be ignored. `tile_count`: the number of used entries of each row of tile_list.
All inputs are finite; a program needn't handle non-finite values.
Results may differ from the reference program's by a relative error of at most 0.012.
The reference program's roundings to bfloat16 on the way (of `prob_b` and `grad_score`) count: a program that leaves them out, or rounds other values in their place, can miss the bound.
Values may be sent and summed in bfloat16 or wider, within the bound.
A program may use at most 128 MiB of HBM per device.

```python
import jax
import jax.numpy as jnp
from jax import lax

HEADS = 24
HD = 128
TH = 4
TW = 2
LIST = 12
D = 3072
TILE = 128
TILES_DEV = 8
NTILES = 256
TOKENS = 32768


def tile_layout(key):
    base = jax.random.fold_in(key, 7)
    frames = NTILES // TILES_DEV
    tiles = jnp.arange(NTILES, dtype=jnp.int32)
    t_pos = tiles // TILES_DEV
    h_pos = tiles // TW % TH
    w_pos = tiles % TW
    offsets = jnp.arange(27, dtype=jnp.int32)
    step_t = offsets // 9 - 1
    step_h = offsets // 3 % 3 - 1
    step_w = offsets % 3 - 1
    near_t = t_pos[:, None] + step_t[None, :]
    near_h = h_pos[:, None] + step_h[None, :]
    near_w = w_pos[:, None] + step_w[None, :]
    inside = (near_t >= 0) & (near_t < frames) & (near_h >= 0) & (near_h < TH) & (near_w >= 0) & (near_w < TW)
    candidate = (near_t * TH + near_h) * TW + near_w
    candidate = jnp.where(inside, candidate, tiles[:, None])
    ranking = jax.random.randint(jax.random.fold_in(base, 1), (NTILES, 27), 0, 1024)
    ranking = jnp.where(offsets[None, :] == 13, 2048, ranking)
    ranking = jnp.where(inside, ranking, -1) * 32 + offsets[None, :]
    _, order = lax.top_k(ranking, LIST)
    lists = jnp.take_along_axis(candidate, order, axis=1)
    level_table = jnp.array([2, 3, 4, 6], jnp.int32)
    level = level_table[jax.random.randint(jax.random.fold_in(base, 2), (frames,), 0, 4)]
    level = level.at[1].set(LIST)
    tile_level = level[t_pos]
    lowest = jnp.maximum(tile_level // 2, 1)
    counts = jax.random.randint(jax.random.fold_in(base, 3), (NTILES,), lowest, tile_level + 1)
    counts = jnp.minimum(counts, jnp.sum(inside.astype(jnp.int32), axis=1))
    counts = counts.at[TILES_DEV + TW].set(LIST).at[0].set(1)
    return (lists.astype(jnp.int32), counts.astype(jnp.int32))


def draw_tile_list(key, part):
    return tile_layout(key)[0]


def draw_tile_count(key, part):
    return tile_layout(key)[1]


def draw_query(key, part):
    drawn = 1.25 * jax.random.truncated_normal(jax.random.fold_in(key, 21), -4.8, 4.8, (TOKENS, D), jnp.float32)
    return drawn.astype(jnp.bfloat16)


def draw_key(key, part):
    drawn = 1.25 * jax.random.truncated_normal(jax.random.fold_in(key, 22), -4.8, 4.8, (TOKENS, D), jnp.float32)
    return drawn.astype(jnp.bfloat16)


def level_of(stream_key, extent, shards, low, high):
    loudness = 1.0
    for position, parts in shards:
        draws = jax.random.uniform(jax.random.fold_in(jax.random.fold_in(stream_key, 6), position), (parts,), jnp.float32, low / len(shards), high / len(shards))
        loudness = loudness * jnp.repeat(jnp.exp(draws), extent[position] // parts).reshape((-1,) + (1,) * (len(extent) - 1 - position))
    return loudness


def normal_values(key, extent, scale, reach, cuts=(), held_as=jnp.bfloat16):
    values = jax.random.normal(key, extent, jnp.float32) * scale
    if len(cuts) > 0:
        values = level_of(key, extent, cuts, -0.22, 0.18) * values
    return jnp.clip(values, min=-reach, max=reach).astype(held_as)


def setup_inputs(seed: int = 0) -> dict:
    streams_of = jax.random.split(jax.random.key(seed), 7)
    query = draw_query(jax.random.fold_in(streams_of[6], 71), 0)
    key = draw_key(jax.random.fold_in(streams_of[6], 71), 0)
    value = normal_values(streams_of[2], (TOKENS, D), 1.0, 6.0, ((0, 256),))
    grad_out = normal_values(streams_of[3], (TOKENS, D), 1.0, 6.0, ((0, 256),))
    tile_list = draw_tile_list(jax.random.fold_in(streams_of[6], 71), 0)
    tile_count = draw_tile_count(jax.random.fold_in(streams_of[6], 71), 0)
    return {"query": query, "key": key, "value": value, "grad_out": grad_out, "tile_list": tile_list, "tile_count": tile_count}


def rounded(values):
    return lax.optimization_barrier(values.astype(jnp.bfloat16)).astype(jnp.float32)


def reference(query, key, value, grad_out, tile_list, tile_count):
    scaling = HD ** -0.5
    query_tiles = query.reshape(NTILES, TILE, HEADS, HD)
    key_tiles = key.reshape(NTILES, TILE, HEADS, HD)
    value_tiles = value.reshape(NTILES, TILE, HEADS, HD)
    cotangent_tiles = grad_out.reshape(NTILES, TILE, HEADS, HD)
    slot_ids = jnp.arange(LIST, dtype=jnp.int32)

    def per_tile(accums, tile_index):
        accum_key, accum_value = accums
        kv_tiles = tile_list[tile_index]
        in_use = slot_ids < tile_count[tile_index]
        relation = (tile_index // TILES_DEV - kv_tiles // TILES_DEV + 1).astype(jnp.int32)
        query_tile = query_tiles[tile_index].astype(jnp.float32)
        cotangent = cotangent_tiles[tile_index].astype(jnp.float32)
        keys_here = key_tiles[kv_tiles].astype(jnp.float32)
        values_here = value_tiles[kv_tiles].astype(jnp.float32)
        score = jnp.einsum('qhd,lkhd->hqlk', query_tile, keys_here) * scaling
        score = jnp.where(in_use[None, None, :, None], score, -jnp.inf)
        row_max = jnp.max(score, axis=(2, 3), keepdims=True)
        log_total = row_max + jnp.log(jnp.sum(jnp.exp(score - row_max), axis=(2, 3), keepdims=True))
        probability = jnp.exp(score - log_total)
        prob_b = lax.optimization_barrier(probability.astype(jnp.bfloat16)).astype(jnp.float32)
        output = jnp.einsum('hqlk,lkhd->qhd', prob_b, values_here).astype(jnp.bfloat16)
        output_wide = lax.optimization_barrier(output).astype(jnp.float32)
        row_delta = jnp.sum(cotangent * output_wide, axis=2)
        grad_prob = jnp.einsum('qhd,lkhd->hqlk', cotangent, values_here)
        grad_score = probability * (grad_prob - row_delta.T[:, :, None, None])
        grad_score = lax.optimization_barrier(grad_score.astype(jnp.bfloat16)).astype(jnp.float32)
        query_grad = (scaling * jnp.einsum('hqlk,lkhd->qhd', grad_score, keys_here)).astype(jnp.bfloat16)
        accum_key = accum_key.at[relation, kv_tiles].add(jnp.einsum('hqlk,qhd->lkhd', grad_score, query_tile))
        accum_value = accum_value.at[relation, kv_tiles].add(jnp.einsum('hqlk,qhd->lkhd', prob_b, cotangent))
        return (accum_key, accum_value), (output, query_grad)

    empty_grads = jnp.zeros((3, NTILES, TILE, HEADS, HD), jnp.float32)
    (accum_key, accum_value), (outputs, query_grads) = lax.scan(
        per_tile, (empty_grads, empty_grads), jnp.arange(NTILES, dtype=jnp.int32))
    attn_out = outputs.reshape(TOKENS, D)
    grad_query = query_grads.reshape(TOKENS, D)
    key_sum = accum_key[1] + rounded(accum_key[0]) + rounded(accum_key[2])
    value_sum = accum_value[1] + rounded(accum_value[0]) + rounded(accum_value[2])
    grad_key = (scaling * key_sum).astype(jnp.bfloat16).reshape(TOKENS, D)
    grad_value = value_sum.astype(jnp.bfloat16).reshape(TOKENS, D)
    return (attn_out, grad_query, grad_key, grad_value)
```

```python
import functools

import jax
import jax.numpy as jnp
from jax import lax
from jax.experimental import pallas as pl
from jax.experimental.pallas import tpu as pltpu
from jax.sharding import PartitionSpec as P

HD = 128
TILE = 128
TILES_DEV = 8
SLAB = 1024
LIST = 12
GROUP = 4
CHUNKS = LIST // GROUP
SCALING = HD ** (-0.5)
LOG2E = 1.4426950408889634
UNUSED = 1e30


def attention_kernel(
    heads, list_hbm, count_ref, q_hbm, g_hbm, kp_hbm, vp_hbm,
    o_hbm, dq_hbm, low_hbm, up_hbm, own_hbm,
    list_ref, q_ref, g_ref, kp_ref, vp_ref, w_ref, e_ref, dp_ref, stat_ref, ot_ref, dqt_ref,
    acc_ref, o_ref, dq_ref, low_ref, up_ref, own_ref, in_sem, out_sem,
):
    slab = lax.axis_index("seq")
    loads = [
        pltpu.make_async_copy(src, dst, in_sem.at[i])
        for i, (src, dst) in enumerate(
            [
                (list_hbm.at[pl.ds(pl.multiple_of(slab * TILES_DEV, TILES_DEV), TILES_DEV)], list_ref),
                (kp_hbm, kp_ref),
                (vp_hbm, vp_ref),
                (q_hbm, q_ref),
                (g_hbm, g_ref),
            ]
        )
    ]
    for load in loads:
        load.start()
    w_ref[...] = jnp.zeros_like(w_ref)

    def clear(slot, _):
        acc_ref[slot] = jnp.zeros(acc_ref.shape[1:], jnp.float32)
        return 0

    lax.fori_loop(0, 3 * TILES_DEV, clear, 0)
    for load in loads:
        load.wait()

    def columns(h):
        return slice(h * HD, (h + 1) * HD)

    def query_tile(a, _):
        used = count_ref[slab * TILES_DEV + a]
        chunks = (used + (GROUP - 1)) // GROUP
        for h in range(heads):
            w_ref[h, :TILE, :HD] = g_ref[a, :, columns(h)]
            w_ref[h, TILE:, HD:] = q_ref[a, :, columns(h)]
        ot_ref[...] = jnp.zeros_like(ot_ref)
        dqt_ref[...] = jnp.zeros_like(dqt_ref)
        for c in range(CHUNKS):
            stat_ref[c] = jnp.full(stat_ref.shape[1:], -UNUSED, jnp.float32)

        def slots_of(c):
            slots, extra = [], []
            for u in range(GROUP):
                j = c * GROUP + u
                valid = j < used
                slots.append(list_ref[a, jnp.where(valid, j, 0)] - (slab - 1) * TILES_DEV)
                extra.append(jnp.where(valid, 0.0, UNUSED).astype(jnp.float32))
            return slots, extra

        def scores(c, _):
            slots, extra = slots_of(c)
            for h in range(heads):
                pairs = jnp.concatenate(
                    [
                        jnp.concatenate([vp_ref[s, :, columns(h)], kp_ref[s, :, columns(h)]], axis=1)
                        for s in slots
                    ],
                    axis=0,
                )
                both = lax.dot_general(
                    pairs, w_ref[h], (((1,), (1,)), ((), ())), preferred_element_type=jnp.float32
                )
                grad_prob = both[:, :TILE]
                score = both[:, TILE:]
                top = jnp.max(score, axis=0, keepdims=True)
                total = jnp.zeros((1, TILE), jnp.float32)
                dots = jnp.zeros((1, TILE), jnp.float32)
                for u in range(GROUP):
                    rows = slice(u * TILE, (u + 1) * TILE)
                    e = jnp.exp2((score[rows] - (top + extra[u])) * (SCALING * LOG2E))
                    e_ref[c, h, rows] = e
                    total = total + jnp.sum(e, axis=0, keepdims=True)
                    dots = dots + jnp.sum(e * grad_prob[rows], axis=0, keepdims=True)
                dp_ref[c, h] = grad_prob
                stat_ref[c, h, 0:1] = top
                stat_ref[c, h, 1:2] = total
                stat_ref[c, h, 2:3] = dots
            return 0

        lax.fori_loop(0, chunks, scores, 0)

        for h in range(heads):
            top = functools.reduce(jnp.maximum, [stat_ref[c, h, 0:1] for c in range(CHUNKS)])
            total = jnp.zeros((1, TILE), jnp.float32)
            dots = jnp.zeros((1, TILE), jnp.float32)
            weights = []
            for c in range(CHUNKS):
                weight = jnp.exp2((stat_ref[c, h, 0:1] - top) * (SCALING * LOG2E))
                total = total + weight * stat_ref[c, h, 1:2]
                dots = dots + weight * stat_ref[c, h, 2:3]
                weights.append(weight)
            inverse = 1.0 / total
            for c in range(CHUNKS):
                stat_ref[c, h, 3:4] = weights[c] * inverse
            stat_ref[0, h, 4:5] = dots * inverse

        def grads(c, _):
            slots, _ = slots_of(c)
            for h in range(heads):
                factor = stat_ref[c, h, 3:4]
                delta = stat_ref[0, h, 4:5]
                p = e_ref[c, h] * factor
                ds = (p * (dp_ref[c, h] - delta)).astype(jnp.bfloat16)
                pb = p.astype(jnp.bfloat16)
                keys = jnp.concatenate([kp_ref[s, :, columns(h)] for s in slots], axis=0)
                values = jnp.concatenate([vp_ref[s, :, columns(h)] for s in slots], axis=0)
                both = lax.dot_general(
                    jnp.concatenate([pb, ds], axis=1), w_ref[h], (((1,), (0,)), ((), ())),
                    preferred_element_type=jnp.float32,
                )
                for u in range(GROUP):
                    acc_ref[slots[u], :, 2 * h * HD : 2 * (h + 1) * HD] += both[u * TILE : (u + 1) * TILE]
                ot_ref[h] += lax.dot_general(
                    values, pb, (((0,), (0,)), ((), ())), preferred_element_type=jnp.float32
                )
                dqt_ref[h] += lax.dot_general(
                    keys, ds, (((0,), (0,)), ((), ())), preferred_element_type=jnp.float32
                )
            return 0

        lax.fori_loop(0, chunks, grads, 0)
        for h in range(heads):
            o_ref[a, :, columns(h)] = ot_ref[h].T.astype(jnp.bfloat16)
            dq_ref[a, :, columns(h)] = (dqt_ref[h].T * SCALING).astype(jnp.bfloat16)
        return 0

    lax.fori_loop(0, TILES_DEV, query_tile, 0)

    stores = [
        pltpu.make_async_copy(src, dst, out_sem.at[i])
        for i, (src, dst) in enumerate(
            [(o_ref, o_hbm), (dq_ref, dq_hbm), (low_ref, low_hbm), (up_ref, up_hbm), (own_ref, own_hbm)]
        )
    ]
    stores[0].start()
    stores[1].start()

    def finish(t, _):
        for h in range(heads):
            for kind in range(2):
                part = slice((2 * h + 1 - kind) * HD, (2 * h + 2 - kind) * HD)
                low_ref[kind, t, :, columns(h)] = acc_ref[t, :, part].astype(jnp.bfloat16)
                up_ref[kind, t, :, columns(h)] = acc_ref[2 * TILES_DEV + t, :, part].astype(jnp.bfloat16)
                own_ref[kind, t, :, columns(h)] = acc_ref[TILES_DEV + t, :, part]
        return 0

    lax.fori_loop(0, TILES_DEV, finish, 0)
    for store in stores[2:]:
        store.start()
    for store in stores:
        store.wait()


def attention(tile_list, tile_count, query, cotangent, key_pool, value_pool):
    columns = query.shape[2]
    heads = columns // HD
    own = (TILES_DEV, TILE, columns)
    pool = (3 * TILES_DEV, TILE, columns)
    pair = (2,) + own
    hbm = pl.BlockSpec(memory_space=pl.ANY)
    outs = (
        jax.ShapeDtypeStruct(own, jnp.bfloat16),
        jax.ShapeDtypeStruct(own, jnp.bfloat16),
        jax.ShapeDtypeStruct(pair, jnp.bfloat16),
        jax.ShapeDtypeStruct(pair, jnp.bfloat16),
        jax.ShapeDtypeStruct(pair, jnp.float32),
    )
    wide = (CHUNKS, heads, GROUP * TILE, TILE)
    return pl.pallas_call(
        functools.partial(attention_kernel, heads),
        out_shape=outs,
        in_specs=[hbm, pl.BlockSpec(memory_space=pltpu.SMEM), hbm, hbm, hbm, hbm],
        out_specs=(hbm,) * 5,
        scratch_shapes=[
            pltpu.SMEM((TILES_DEV, LIST), jnp.int32),
            pltpu.VMEM(own, jnp.bfloat16),
            pltpu.VMEM(own, jnp.bfloat16),
            pltpu.VMEM(pool, jnp.bfloat16),
            pltpu.VMEM(pool, jnp.bfloat16),
            pltpu.VMEM((heads, 2 * TILE, 2 * HD), jnp.bfloat16),
            pltpu.VMEM(wide, jnp.float32),
            pltpu.VMEM(wide, jnp.float32),
            pltpu.VMEM((CHUNKS, heads, 8, TILE), jnp.float32),
            pltpu.VMEM((heads, HD, TILE), jnp.float32),
            pltpu.VMEM((heads, HD, TILE), jnp.float32),
            pltpu.VMEM((3 * TILES_DEV, TILE, 2 * columns), jnp.float32),
            pltpu.VMEM(own, jnp.bfloat16),
            pltpu.VMEM(own, jnp.bfloat16),
            pltpu.VMEM(pair, jnp.bfloat16),
            pltpu.VMEM(pair, jnp.bfloat16),
            pltpu.VMEM(pair, jnp.float32),
            pltpu.SemaphoreType.DMA((5,)),
            pltpu.SemaphoreType.DMA((5,)),
        ],
        compiler_params=pltpu.CompilerParams(vmem_limit_bytes=56 * 2**20),
        name="attention",
    )(tile_list, tile_count, query, cotangent, key_pool, value_pool)


def with_rims(cells):
    count = lax.axis_size("seq")
    ring = range(count)
    return jnp.concatenate(
        [
            lax.ppermute(cells, "seq", [(i, (i + 1) % count) for i in ring]),
            cells,
            lax.ppermute(cells, "seq", [((i + 1) % count, i) for i in ring]),
        ],
        axis=0,
    )


def per_device(query, key, value, grad_out, tile_list, tile_count):
    def gathered(cells):
        moved = lax.all_to_all(cells, "head", split_axis=1, concat_axis=0, tiled=True)
        return moved.reshape(TILES_DEV, TILE, moved.shape[1])

    def returned(cells):
        return lax.all_to_all(cells.reshape(SLAB, -1), "head", split_axis=0, concat_axis=1, tiled=True)

    key_pool = with_rims(gathered(key))
    value_pool = with_rims(gathered(value))
    out, dq, low, up, own = attention(
        tile_list, tile_count, gathered(query), gathered(grad_out), key_pool, value_pool
    )
    count = lax.axis_size("seq")
    ring = range(count)
    from_below = lax.ppermute(up, "seq", [(i, (i + 1) % count) for i in ring])
    from_above = lax.ppermute(low, "seq", [((i + 1) % count, i) for i in ring])
    total = own + from_below.astype(jnp.float32) + from_above.astype(jnp.float32)
    dk = (SCALING * total[0]).astype(jnp.bfloat16)
    dv = total[1].astype(jnp.bfloat16)
    return returned(out), returned(dq), returned(dk), returned(dv)


def solution(mesh):
    tokens = P(("seq", "head"), None)
    return jax.shard_map(
        per_device,
        mesh=mesh,
        in_specs=(tokens, tokens, tokens, tokens, P(), P()),
        out_specs=(tokens, tokens, tokens, tokens),
        check_vma=False,
    )
```

```python
import functools

import jax
import jax.numpy as jnp
from jax import lax
from jax.experimental import pallas as pl
from jax.experimental.pallas import tpu as pltpu
from jax.sharding import PartitionSpec as P

HD = 128
TILE = 128
TILES_DEV = 8
SLAB = 1024
LIST = 12
GROUP = 4
CHUNKS = LIST // GROUP
SCALING = HD ** (-0.5)
LOG2E = 1.4426950408889634
UNUSED = 1e30


def attention_kernel(
    heads, list_hbm, count_ref, q_hbm, g_hbm, kp_hbm, vp_hbm,
    o_hbm, dq_hbm, low_hbm, up_hbm, own_hbm,
    list_ref, q_ref, g_ref, kp_ref, vp_ref, w_ref, e_ref, dp_ref, stat_ref, ot_ref, dqt_ref,
    acc_ref, o_ref, dq_ref, low_ref, up_ref, own_ref, in_sem, out_sem,
):
    slab = lax.axis_index("seq")
    loads = [
        pltpu.make_async_copy(src, dst, in_sem.at[i])
        for i, (src, dst) in enumerate(
            [
                (list_hbm, list_ref),
                (kp_hbm, kp_ref),
                (vp_hbm, vp_ref),
                (q_hbm, q_ref),
                (g_hbm, g_ref),
            ]
        )
    ]
    for load in loads:
        load.start()
    w_ref[...] = jnp.zeros_like(w_ref)

    def clear(slot, _):
        acc_ref[slot] = jnp.zeros(acc_ref.shape[1:], jnp.float32)
        return 0

    lax.fori_loop(0, 3 * TILES_DEV, clear, 0)
    for load in loads:
        load.wait()

    def columns(h):
        return slice(h * HD, (h + 1) * HD)

    def query_tile(a, _):
        used = count_ref[slab * TILES_DEV + a]
        chunks = (used + (GROUP - 1)) // GROUP
        for h in range(heads):
            w_ref[h, :TILE, :HD] = g_ref[a, :, columns(h)]
            w_ref[h, TILE:, HD:] = q_ref[a, :, columns(h)]
        ot_ref[...] = jnp.zeros_like(ot_ref)
        dqt_ref[...] = jnp.zeros_like(dqt_ref)
        for c in range(CHUNKS):
            stat_ref[c] = jnp.full(stat_ref.shape[1:], -UNUSED, jnp.float32)

        def slots_of(c):
            slots, extra = [], []
            for u in range(GROUP):
                j = c * GROUP + u
                valid = j < used
                slots.append(list_ref[jnp.where(valid, j, 0), slab * TILES_DEV + a] - (slab - 1) * TILES_DEV)
                extra.append(jnp.where(valid, 0.0, UNUSED).astype(jnp.float32))
            return slots, extra

        def scores(c, _):
            slots, extra = slots_of(c)
            for h in range(heads):
                pairs = jnp.concatenate(
                    [
                        jnp.concatenate([vp_ref[s, :, columns(h)], kp_ref[s, :, columns(h)]], axis=1)
                        for s in slots
                    ],
                    axis=0,
                )
                both = lax.dot_general(
                    pairs, w_ref[h], (((1,), (1,)), ((), ())), preferred_element_type=jnp.float32
                )
                grad_prob = both[:, :TILE]
                score = both[:, TILE:]
                top = jnp.max(score, axis=0, keepdims=True)
                total = jnp.zeros((1, TILE), jnp.float32)
                dots = jnp.zeros((1, TILE), jnp.float32)
                for u in range(GROUP):
                    rows = slice(u * TILE, (u + 1) * TILE)
                    e = jnp.exp2((score[rows] - (top + extra[u])) * (SCALING * LOG2E))
                    e_ref[c, h, rows] = e
                    total = total + jnp.sum(e, axis=0, keepdims=True)
                    dots = dots + jnp.sum(e * grad_prob[rows], axis=0, keepdims=True)
                dp_ref[c, h] = grad_prob
                stat_ref[c, h, 0:1] = top
                stat_ref[c, h, 1:2] = total
                stat_ref[c, h, 2:3] = dots
            return 0

        lax.fori_loop(0, chunks, scores, 0)

        for h in range(heads):
            top = functools.reduce(jnp.maximum, [stat_ref[c, h, 0:1] for c in range(CHUNKS)])
            total = jnp.zeros((1, TILE), jnp.float32)
            dots = jnp.zeros((1, TILE), jnp.float32)
            weights = []
            for c in range(CHUNKS):
                weight = jnp.exp2((stat_ref[c, h, 0:1] - top) * (SCALING * LOG2E))
                total = total + weight * stat_ref[c, h, 1:2]
                dots = dots + weight * stat_ref[c, h, 2:3]
                weights.append(weight)
            inverse = 1.0 / total
            for c in range(CHUNKS):
                stat_ref[c, h, 3:4] = weights[c] * inverse
            stat_ref[0, h, 4:5] = dots * inverse

        def grads(c, _):
            slots, _ = slots_of(c)
            for h in range(heads):
                factor = stat_ref[c, h, 3:4]
                delta = stat_ref[0, h, 4:5]
                p = e_ref[c, h] * factor
                ds = (p * (dp_ref[c, h] - delta)).astype(jnp.bfloat16)
                pb = p.astype(jnp.bfloat16)
                keys = jnp.concatenate([kp_ref[s, :, columns(h)] for s in slots], axis=0)
                values = jnp.concatenate([vp_ref[s, :, columns(h)] for s in slots], axis=0)
                both = lax.dot_general(
                    jnp.concatenate([pb, ds], axis=1), w_ref[h], (((1,), (0,)), ((), ())),
                    preferred_element_type=jnp.float32,
                )
                for u in range(GROUP):
                    acc_ref[slots[u], :, 2 * h * HD : 2 * (h + 1) * HD] += both[u * TILE : (u + 1) * TILE]
                ot_ref[h] += lax.dot_general(
                    values, pb, (((0,), (0,)), ((), ())), preferred_element_type=jnp.float32
                )
                dqt_ref[h] += lax.dot_general(
                    keys, ds, (((0,), (0,)), ((), ())), preferred_element_type=jnp.float32
                )
            return 0

        lax.fori_loop(0, chunks, grads, 0)
        for h in range(heads):
            o_ref[a, :, columns(h)] = ot_ref[h].T.astype(jnp.bfloat16)
            dq_ref[a, :, columns(h)] = (dqt_ref[h].T * SCALING).astype(jnp.bfloat16)
        return 0

    lax.fori_loop(0, TILES_DEV, query_tile, 0)

    stores = [
        pltpu.make_async_copy(src, dst, out_sem.at[i])
        for i, (src, dst) in enumerate(
            [(o_ref, o_hbm), (dq_ref, dq_hbm), (low_ref, low_hbm), (up_ref, up_hbm), (own_ref, own_hbm)]
        )
    ]
    stores[0].start()
    stores[1].start()

    def finish(t, _):
        for h in range(heads):
            for kind in range(2):
                part = slice((2 * h + 1 - kind) * HD, (2 * h + 2 - kind) * HD)
                low_ref[t, kind, :, columns(h)] = acc_ref[t, :, part].astype(jnp.bfloat16)
                up_ref[t, kind, :, columns(h)] = acc_ref[2 * TILES_DEV + t, :, part].astype(jnp.bfloat16)
                own_ref[t, kind, :, columns(h)] = acc_ref[TILES_DEV + t, :, part]
        return 0

    lax.fori_loop(0, TILES_DEV, finish, 0)
    for store in stores[2:]:
        store.start()
    for store in stores:
        store.wait()


def attention(tile_list, tile_count, query, cotangent, key_pool, value_pool):
    columns = query.shape[2]
    heads = columns // HD
    own = (TILES_DEV, TILE, columns)
    pool = (3 * TILES_DEV, TILE, columns)
    pair = (TILES_DEV, 2, TILE, columns)
    hbm = pl.BlockSpec(memory_space=pl.ANY)
    outs = (
        jax.ShapeDtypeStruct(own, jnp.bfloat16),
        jax.ShapeDtypeStruct(own, jnp.bfloat16),
        jax.ShapeDtypeStruct(pair, jnp.bfloat16),
        jax.ShapeDtypeStruct(pair, jnp.bfloat16),
        jax.ShapeDtypeStruct(pair, jnp.float32),
    )
    wide = (CHUNKS, heads, GROUP * TILE, TILE)
    return pl.pallas_call(
        functools.partial(attention_kernel, heads),
        out_shape=outs,
        in_specs=[hbm, pl.BlockSpec(memory_space=pltpu.SMEM), hbm, hbm, hbm, hbm],
        out_specs=(hbm,) * 5,
        scratch_shapes=[
            pltpu.SMEM(tile_list.shape, jnp.int32),
            pltpu.VMEM(own, jnp.bfloat16),
            pltpu.VMEM(own, jnp.bfloat16),
            pltpu.VMEM(pool, jnp.bfloat16),
            pltpu.VMEM(pool, jnp.bfloat16),
            pltpu.VMEM((heads, 2 * TILE, 2 * HD), jnp.bfloat16),
            pltpu.VMEM(wide, jnp.float32),
            pltpu.VMEM(wide, jnp.float32),
            pltpu.VMEM((CHUNKS, heads, 8, TILE), jnp.float32),
            pltpu.VMEM((heads, HD, TILE), jnp.float32),
            pltpu.VMEM((heads, HD, TILE), jnp.float32),
            pltpu.VMEM((3 * TILES_DEV, TILE, 2 * columns), jnp.float32),
            pltpu.VMEM(own, jnp.bfloat16),
            pltpu.VMEM(own, jnp.bfloat16),
            pltpu.VMEM(pair, jnp.bfloat16),
            pltpu.VMEM(pair, jnp.bfloat16),
            pltpu.VMEM(pair, jnp.float32),
            pltpu.SemaphoreType.DMA((5,)),
            pltpu.SemaphoreType.DMA((5,)),
        ],
        compiler_params=pltpu.CompilerParams(vmem_limit_bytes=56 * 2**20),
        name="attention",
    )(tile_list, tile_count, query, cotangent, key_pool, value_pool)


MESH = pl.DeviceIdType.MESH


def swapped(head, flag):
    return head + flag * (1 - 2 * lax.rem(head, 2))


def placement():
    slabs = lax.axis_size("seq")
    slab, head = lax.axis_index("seq"), lax.axis_index("head")
    above, below = lax.rem(slab + 1, slabs), lax.rem(slab + slabs - 1, slabs)

    def flag(s):
        return lax.rem(lax.div(s, 2), 2)

    own = flag(slab)
    head_above = swapped(head, lax.rem(own + flag(above), 2))
    head_below = swapped(head, lax.rem(own + flag(below), 2))
    return slab, head, own, (above, head_above), (below, head_below)


def entry_barrier(slab, head, heads, neighbours):
    barrier = pltpu.get_barrier_semaphore()

    def greet(r, _):
        pl.semaphore_signal(
            barrier, inc=1, device_id={"seq": slab, "head": lax.rem(head + r, heads)}, device_id_type=MESH
        )
        return 0

    lax.fori_loop(1, heads, greet, 0)
    for s, h in neighbours:
        pl.semaphore_signal(barrier, inc=1, device_id={"seq": s, "head": h}, device_id_type=MESH)
    pl.semaphore_wait(barrier, heads - 1 + len(neighbours))


def gather_kernel(
    k_hbm, v_hbm, q_hbm, g_hbm, kp_hbm, vp_hbm, qo_hbm, go_hbm,
    local_sem, send_sem, recv_sem, rim_send, rim_recv,
):
    heads = lax.axis_size("head")
    slab, head, flag, above, below = placement()
    width = qo_hbm.shape[2]
    entry_barrier(slab, head, heads, (above, below))
    streams = [
        (k_hbm, kp_hbm, TILES_DEV), (v_hbm, vp_hbm, TILES_DEV), (q_hbm, qo_hbm, 0), (g_hbm, go_hbm, 0)
    ]

    def block(i, peer):
        group = swapped(peer, flag)
        return streams[i][0].at[:, pl.ds(pl.multiple_of(group * width, width), width)]

    def local(i):
        _, dst, base = streams[i]
        return pltpu.make_async_copy(block(i, head), dst.at[base + head], local_sem.at[i])

    def exchange(i, peer, slot):
        _, dst, base = streams[i]
        return pltpu.make_async_remote_copy(
            src_ref=block(i, peer),
            dst_ref=dst.at[base + slot],
            send_sem=send_sem.at[i, peer],
            recv_sem=recv_sem.at[i, slot],
            device_id={"seq": slab, "head": peer},
            device_id_type=MESH,
        )

    def rim(i, side, tile):
        dst = streams[i][1]
        s, h = (above, below)[side]
        return pltpu.make_async_remote_copy(
            src_ref=dst.at[TILES_DEV + tile],
            dst_ref=dst.at[2 * TILES_DEV * side + tile],
            send_sem=rim_send.at[i, side, tile],
            recv_sem=rim_recv.at[i, side, tile],
            device_id={"seq": s, "head": h},
            device_id_type=MESH,
        )

    def peers(body):
        def step(r, _):
            body(lax.rem(head + r, heads))
            return 0

        lax.fori_loop(1, heads, step, 0)

    def send_all(i):
        local(i).start()
        peers(lambda peer: exchange(i, peer, head).start())

    def forward(i):
        local(i).wait()
        rim(i, 0, head).start()
        rim(i, 1, head).start()

        def arrived(peer):
            exchange(i, peer, peer).wait_recv()
            rim(i, 0, peer).start()
            rim(i, 1, peer).start()

        peers(arrived)

    send_all(0)
    send_all(1)
    forward(0)
    send_all(2)
    forward(1)
    send_all(3)
    for i in (2, 3):
        local(i).wait()
        peers(lambda peer: exchange(i, peer, peer).wait_recv())
    for i in range(4):
        peers(lambda peer: exchange(i, peer, head).wait_send())

    def settle(tile, _):
        for i in range(2):
            for side in range(2):
                rim(i, side, tile).wait_recv()
                rim(i, side, tile).wait_send()
        return 0

    lax.fori_loop(0, TILES_DEV, settle, 0)


def gather(key, value, query, cotangent):
    columns = key.shape[1] // TILES_DEV
    hbm = pl.BlockSpec(memory_space=pl.ANY)
    own = jax.ShapeDtypeStruct((TILES_DEV, TILE, columns), jnp.bfloat16)
    pool = jax.ShapeDtypeStruct((3 * TILES_DEV, TILE, columns), jnp.bfloat16)
    return pl.pallas_call(
        gather_kernel,
        out_shape=(pool, pool, own, own),
        in_specs=[hbm] * 4,
        out_specs=(hbm,) * 4,
        scratch_shapes=[
            pltpu.SemaphoreType.DMA((4,)),
            pltpu.SemaphoreType.DMA((4, TILES_DEV)),
            pltpu.SemaphoreType.DMA((4, TILES_DEV)),
            pltpu.SemaphoreType.DMA((2, 2, TILES_DEV)),
            pltpu.SemaphoreType.DMA((2, 2, TILES_DEV)),
        ],
        compiler_params=pltpu.CompilerParams(collective_id=0, has_side_effects=True),
        name="gather",
    )(key, value, query, cotangent)


def scatter_kernel(
    o_hbm, dq_hbm, low_hbm, up_hbm, own_hbm, oo_hbm, dqo_hbm, dko_hbm, dvo_hbm,
    own_ref, from_below, from_above, dk_ref, dv_ref,
    own_sem, local_sem, send_sem, recv_sem, rim_send, rim_recv,
):
    heads = lax.axis_size("head")
    slab, head, flag, above, below = placement()
    width = o_hbm.shape[2]
    columns = pl.ds(pl.multiple_of(swapped(head, flag) * width, width), width)
    own_load = pltpu.make_async_copy(own_hbm, own_ref, own_sem)
    own_load.start()
    entry_barrier(slab, head, heads, (above, below))

    def rim(side, tile):
        s, h = (above, below)[side]
        return pltpu.make_async_remote_copy(
            src_ref=(up_hbm, low_hbm)[side].at[tile],
            dst_ref=(from_below, from_above)[side].at[tile],
            send_sem=rim_send.at[side, tile],
            recv_sem=rim_recv.at[side, tile],
            device_id={"seq": s, "head": h},
            device_id_type=MESH,
        )

    streams = [(o_hbm, oo_hbm), (dq_hbm, dqo_hbm), (dk_ref, dko_hbm), (dv_ref, dvo_hbm)]

    def local(i):
        src, dst = streams[i]
        return pltpu.make_async_copy(src.at[head], dst.at[:, columns], local_sem.at[i])

    def exchange(i, peer, slot):
        src, dst = streams[i]
        return pltpu.make_async_remote_copy(
            src_ref=src.at[peer],
            dst_ref=dst.at[:, columns],
            send_sem=send_sem.at[i, peer],
            recv_sem=recv_sem.at[i, slot],
            device_id={"seq": slab, "head": peer},
            device_id_type=MESH,
        )

    def peers(body):
        def step(r, _):
            body(lax.rem(head + r, heads))
            return 0

        lax.fori_loop(1, heads, step, 0)

    def start_rims(r, _):
        for side, (_, h) in enumerate((above, below)):
            rim(side, lax.rem(h + r, heads)).start()
        return 0

    lax.fori_loop(1, heads + 1, start_rims, 0)
    for i in range(2):
        peers(lambda peer: exchange(i, peer, head).start())
        local(i).start()
    own_load.wait()

    def summed(tile):
        rim(0, tile).wait_recv()
        rim(1, tile).wait_recv()
        for kind, (ref, factor) in enumerate(((dk_ref, SCALING), (dv_ref, None))):
            total = (
                own_ref[tile, kind]
                + from_below[tile, kind].astype(jnp.float32)
                + from_above[tile, kind].astype(jnp.float32)
            )
            if factor is not None:
                total = factor * total
            ref[tile] = total.astype(jnp.bfloat16)

    def finish(peer):
        summed(peer)
        exchange(2, peer, head).start()
        exchange(3, peer, head).start()

    peers(finish)
    summed(head)
    local(2).start()
    local(3).start()

    def settle(peer):
        for i in range(4):
            exchange(i, peer, peer).wait_recv()
            exchange(i, peer, head).wait_send()

    peers(settle)
    for i in range(4):
        local(i).wait()

    def settle_rims(tile, _):
        rim(0, tile).wait_send()
        rim(1, tile).wait_send()
        return 0

    lax.fori_loop(0, TILES_DEV, settle_rims, 0)


def scatter(out, dq, low, up, own):
    width = out.shape[2]
    hbm = pl.BlockSpec(memory_space=pl.ANY)
    tokens = jax.ShapeDtypeStruct((TILE, TILES_DEV * width), jnp.bfloat16)
    rims = (TILES_DEV, 2, TILE, width)
    return pl.pallas_call(
        scatter_kernel,
        out_shape=(tokens,) * 4,
        in_specs=[hbm] * 5,
        out_specs=(hbm,) * 4,
        scratch_shapes=[
            pltpu.VMEM(rims, jnp.float32),
            pltpu.VMEM(rims, jnp.bfloat16),
            pltpu.VMEM(rims, jnp.bfloat16),
            pltpu.VMEM((TILES_DEV, TILE, width), jnp.bfloat16),
            pltpu.VMEM((TILES_DEV, TILE, width), jnp.bfloat16),
            pltpu.SemaphoreType.DMA(()),
            pltpu.SemaphoreType.DMA((4,)),
            pltpu.SemaphoreType.DMA((4, TILES_DEV)),
            pltpu.SemaphoreType.DMA((4, TILES_DEV)),
            pltpu.SemaphoreType.DMA((2, TILES_DEV)),
            pltpu.SemaphoreType.DMA((2, TILES_DEV)),
        ],
        compiler_params=pltpu.CompilerParams(
            collective_id=1, has_side_effects=True, vmem_limit_bytes=32 * 2**20
        ),
        name="scatter",
    )(out, dq, low, up, own)


def per_device(query, key, value, grad_out, tile_list, tile_count):
    key_pool, value_pool, queries, cotangents = gather(key, value, query, grad_out)
    parts = attention(tile_list.T, tile_count, queries, cotangents, key_pool, value_pool)
    return tuple(scatter(*parts))


def solution(mesh):
    tokens = P(("seq", "head"), None)
    return jax.shard_map(
        per_device,
        mesh=mesh,
        in_specs=(tokens, tokens, tokens, tokens, P(), P()),
        out_specs=(tokens, tokens, tokens, tokens),
        check_vma=False,
    )
```

```python
import functools

import jax
import jax.numpy as jnp
from jax import lax
from jax.experimental import pallas as pl
from jax.experimental.pallas import tpu as pltpu
from jax.sharding import PartitionSpec as P

HD = 128
TILE = 128
TILES_DEV = 8
FRAMES = 3
POOL = FRAMES * TILES_DEV
LIST = 12
SCALING = HD ** (-0.5)
LOG2E = 1.4426950408889634
UNUSED = 1e30
MESH = pl.DeviceIdType.MESH


def swapped(head, flag):
    return head + flag * (1 - 2 * lax.rem(head, 2))


def placement():
    slabs = lax.axis_size("seq")
    slab, head = lax.axis_index("seq"), lax.axis_index("head")
    above, below = lax.rem(slab + 1, slabs), lax.rem(slab + slabs - 1, slabs)

    def flag(s):
        return lax.rem(lax.div(s, 2), 2)

    own = flag(slab)
    head_above = swapped(head, lax.rem(own + flag(above), 2))
    head_below = swapped(head, lax.rem(own + flag(below), 2))
    return slab, head, own, (above, head_above), (below, head_below)


def entry_barrier(slab, head, devices, neighbours):
    barrier = pltpu.get_barrier_semaphore()

    def greet(r, _):
        pl.semaphore_signal(
            barrier, inc=1, device_id={"seq": slab, "head": lax.rem(head + r, devices)}, device_id_type=MESH
        )
        return 0

    lax.fori_loop(1, devices, greet, 0)
    for s, h in neighbours:
        pl.semaphore_signal(barrier, inc=1, device_id={"seq": s, "head": h}, device_id_type=MESH)
    pl.semaphore_wait(barrier, devices - 1 + len(neighbours))


def folded(op, rows):
    return functools.reduce(op, [rows[r : r + 8] for r in range(0, rows.shape[0], 8)])


def fused_kernel(
    heads,
    list_ref, count_ref, k_hbm, v_hbm, q_hbm, g_hbm,
    o_out, dq_out, dk_out, dv_out,
    kv_ref, q_ref, g_ref, acc_ref, mask_ref, w_ref, e_ref, dp_ref, stat_ref, ot_ref, dqt_ref,
    o_ref, dq_ref, dk_ref, dv_ref, low_ref, up_ref, from_below, from_above,
    local_sem, kv_recv, qg_recv, in_send, rim_recv, rim_send,
    out_local, out_send, out_recv, part_recv, part_send,
):
    devices = lax.axis_size("head")
    slab, head, flag, above, below = placement()
    sources = (v_hbm, k_hbm, q_hbm, g_hbm)
    results = ((o_ref, o_out), (dq_ref, dq_out), (dk_ref, dk_out), (dv_ref, dv_out))

    def columns(group, i):
        return pl.ds(pl.multiple_of((group * heads + i) * HD, HD), HD)

    def landing(x, i, slot):
        return kv_ref.at[i, TILES_DEV + slot, x] if x < 2 else (q_ref, g_ref)[x - 2].at[i, slot]

    def local(x, i):
        return pltpu.make_async_copy(
            sources[x].at[:, columns(swapped(head, flag), i)], landing(x, i, head), local_sem.at[i, x]
        )

    def incoming(x, i, peer, slot):
        return pltpu.make_async_remote_copy(
            src_ref=sources[x].at[:, columns(swapped(peer, flag), i)],
            dst_ref=landing(x, i, slot),
            send_sem=in_send.at[i, x],
            recv_sem=kv_recv.at[i, x, slot] if x < 2 else qg_recv.at[i, x - 2],
            device_id={"seq": slab, "head": peer},
            device_id_type=MESH,
        )

    def whole(ref, send_sem, recv_sem):
        return pltpu.make_async_remote_copy(
            src_ref=ref, dst_ref=ref, send_sem=send_sem, recv_sem=recv_sem,
            device_id={"seq": above[0], "head": above[1]}, device_id_type=MESH,
        )

    def rim(i, side, tile):
        s, h = (above, below)[side]
        return pltpu.make_async_remote_copy(
            src_ref=kv_ref.at[i, TILES_DEV + tile],
            dst_ref=kv_ref.at[i, 2 * TILES_DEV * side + tile],
            send_sem=rim_send.at[i, side],
            recv_sem=rim_recv.at[i, side],
            device_id={"seq": s, "head": h},
            device_id_type=MESH,
        )

    def part(i, side, tile):
        s, h = (above, below)[side]
        return pltpu.make_async_remote_copy(
            src_ref=(up_ref, low_ref)[side].at[i, tile],
            dst_ref=(from_below, from_above)[side].at[i, tile],
            send_sem=part_send.at[i, side],
            recv_sem=part_recv.at[i, side, tile],
            device_id={"seq": s, "head": h},
            device_id_type=MESH,
        )

    def result_local(x, i):
        src, dst = results[x]
        return pltpu.make_async_copy(
            src.at[i, head], dst.at[:, columns(swapped(head, flag), i)], out_local.at[i, x]
        )

    def result(x, i, peer):
        src, dst = results[x]
        return pltpu.make_async_remote_copy(
            src_ref=src.at[i, peer],
            dst_ref=dst.at[:, columns(swapped(head, flag), i)],
            send_sem=out_send.at[i, x],
            recv_sem=out_recv.at[i, x],
            device_id={"seq": slab, "head": peer},
            device_id_type=MESH,
        )

    def peers(body):
        def step(r, _):
            body(lax.rem(head + r, devices))
            return 0

        lax.fori_loop(1, devices, step, 0)

    def send(i, streams):
        def both(peer):
            for x in streams:
                incoming(x, i, peer, head).start()

        peers(both)

    def forward(i, r):
        tile = lax.rem(head + r, devices)

        @pl.when(r == 0)
        def _():
            local(0, i).wait()
            local(1, i).wait()

        @pl.when(r > 0)
        def _():
            incoming(0, i, tile, tile).wait_recv()
            incoming(1, i, tile, tile).wait_recv()

        rim(i, 0, tile).start()
        rim(i, 1, tile).start()

    def finish(i, r):
        tile = lax.rem(head + r, devices)
        part(i, 0, tile).wait_recv()
        part(i, 1, tile).wait_recv()
        dv = acc_ref[i, TILES_DEV + tile, :, :HD] + (
            from_below[i, tile, 0].astype(jnp.float32) + from_above[i, tile, 0].astype(jnp.float32)
        )
        dk = acc_ref[i, TILES_DEV + tile, :, HD:] + (
            from_below[i, tile, 1].astype(jnp.float32) + from_above[i, tile, 1].astype(jnp.float32)
        )
        dk_ref[i, tile] = (SCALING * dk).astype(jnp.bfloat16)
        dv_ref[i, tile] = dv.astype(jnp.bfloat16)

        @pl.when(r > 0)
        def _():
            result(2, i, tile).start()
            result(3, i, tile).start()

        @pl.when(r == 0)
        def _():
            result_local(2, i).start()
            result_local(3, i).start()

    def service(i, r):
        @pl.when(i < heads - 1)
        def _():
            forward(i + 1, r)

        @pl.when(i == heads - 1)
        def _():
            finish(0, r)

    def attend(i, a, start, count):
        rows = count * TILE
        w_ref[:TILE, :HD] = g_ref[i, a]
        w_ref[TILE:, HD:] = q_ref[i, a]

        def pairs(f):
            first = f * TILES_DEV + start
            values = kv_ref[i, pl.ds(first, count), 0].reshape(rows, HD)
            keys = kv_ref[i, pl.ds(first, count), 1].reshape(rows, HD)
            return first, values, keys

        def scores(f, _):
            first, values, keys = pairs(f)
            both = lax.dot_general(
                jnp.concatenate([values, keys], axis=1), w_ref[...], (((1,), (1,)), ((), ())),
                preferred_element_type=jnp.float32,
            )
            grad_prob = both[:, :TILE]
            score = both[:, TILE:]
            extra = [mask_ref[a * POOL + first + u] for u in range(count)]
            top = functools.reduce(
                jnp.maximum,
                [folded(jnp.maximum, score[u * TILE : (u + 1) * TILE]) - extra[u] for u in range(count)],
            )
            top = jnp.maximum(jnp.max(top, axis=0, keepdims=True), -0.1 * UNUSED)
            total = jnp.zeros((8, TILE), jnp.float32)
            dots = jnp.zeros((8, TILE), jnp.float32)
            for u in range(count):
                at = slice(u * TILE, (u + 1) * TILE)
                e = jnp.exp2((score[at] - (top + extra[u])) * (SCALING * LOG2E))
                e_ref[f, at] = e
                total = total + folded(jnp.add, e)
                dots = dots + folded(jnp.add, e * grad_prob[at])
            dp_ref[f, :rows] = grad_prob
            stat_ref[f, 0:1] = top
            stat_ref[f, 1:2] = jnp.sum(total, axis=0, keepdims=True)
            stat_ref[f, 2:3] = jnp.sum(dots, axis=0, keepdims=True)
            return 0

        lax.fori_loop(0, FRAMES, scores, 0)

        top = functools.reduce(jnp.maximum, [stat_ref[f, 0:1] for f in range(FRAMES)])
        weights = [jnp.exp2((stat_ref[f, 0:1] - top) * (SCALING * LOG2E)) for f in range(FRAMES)]
        total = sum(weights[f] * stat_ref[f, 1:2] for f in range(FRAMES))
        dots = sum(weights[f] * stat_ref[f, 2:3] for f in range(FRAMES))
        inverse = 1.0 / total
        for f in range(FRAMES):
            stat_ref[f, 3:4] = weights[f] * inverse
            stat_ref[f, 4:5] = dots * inverse
        ot_ref[...] = jnp.zeros_like(ot_ref)
        dqt_ref[...] = jnp.zeros_like(dqt_ref)

        def grads(f, _):
            first, values, keys = pairs(f)
            p = e_ref[f, :rows] * stat_ref[f, 3:4]
            ds = (p * (dp_ref[f, :rows] - stat_ref[f, 4:5])).astype(jnp.bfloat16)
            pb = p.astype(jnp.bfloat16)
            both = lax.dot_general(
                jnp.concatenate([pb, ds], axis=1), w_ref[...], (((1,), (0,)), ((), ())),
                preferred_element_type=jnp.float32,
            )
            for u in range(count):
                acc_ref[i, first + u] += both[u * TILE : (u + 1) * TILE]
            ot_ref[...] += lax.dot_general(
                values, pb, (((0,), (0,)), ((), ())), preferred_element_type=jnp.float32
            )
            dqt_ref[...] += lax.dot_general(
                keys, ds, (((0,), (0,)), ((), ())), preferred_element_type=jnp.float32
            )
            return 0

        lax.fori_loop(0, FRAMES, grads, 0)
        o_ref[i, a] = ot_ref[...].T.astype(jnp.bfloat16)
        dq_ref[i, a] = (dqt_ref[...].T * SCALING).astype(jnp.bfloat16)

    for i in range(heads):
        for x in range(4):
            local(x, i).start()
    entry_barrier(slab, head, devices, (above, below))
    send(0, (0, 1))
    forward(0, 0)
    send(0, (2, 3))

    def masks(a, _):
        used = count_ref[slab * TILES_DEV + a]
        listed = [
            jnp.where(j < used, list_ref[j, slab * TILES_DEV + a] - (slab - 1) * TILES_DEV, -1)
            for j in range(LIST)
        ]

        def one(slot, _):
            hit = functools.reduce(jnp.logical_or, [entry == slot for entry in listed])
            mask_ref[a * POOL + slot] = jnp.where(hit, 0.0, UNUSED).astype(jnp.float32)
            return 0

        lax.fori_loop(0, POOL, one, 0)
        return 0

    lax.fori_loop(0, TILES_DEV, masks, 0)
    w_ref[...] = jnp.zeros_like(w_ref)

    def first_tiles(r, _):
        forward(0, r)
        return 0

    lax.fori_loop(1, devices, first_tiles, 0)
    send(1, (0, 1))

    others = pl.ds(0, devices - 1)

    def head_step(i, _):
        def clear(slot, _):
            acc_ref[i, slot] = jnp.zeros((TILE, 2 * HD), jnp.float32)
            return 0

        lax.fori_loop(0, POOL, clear, 0)

        @pl.when(i < heads - 1)
        def _():
            send(i + 1, (2, 3))

        @pl.when(i < heads - 2)
        def _():
            send(i + 2, (0, 1))

        for x in (2, 3):
            local(x, i).wait()
            whole(q_ref.at[i, others], in_send.at[i, x], qg_recv.at[i, x - 2]).wait_recv()
        for side in range(2):
            whole(
                kv_ref.at[i, pl.ds(TILES_DEV, TILES_DEV)], rim_send.at[i, side], rim_recv.at[i, side]
            ).wait_recv()

        def outer(n, _):
            half = lax.div(n, 2)
            attend(i, n + 4 * half, 4 * half, 4)
            service(i, n)
            return 0

        def inner(n, _):
            attend(i, n + 2, 2 * lax.div(n, 2), 6)
            service(i, n + 4)
            return 0

        lax.fori_loop(0, 4, outer, 0)
        lax.fori_loop(0, 4, inner, 0)

        def leave(r, _):
            for side, (ref, (_, h)) in enumerate(((up_ref, above), (low_ref, below))):
                tile = lax.rem(h + 1 + r, devices)
                for kind in range(2):
                    ref[i, tile, kind] = acc_ref[
                        i, 2 * TILES_DEV * (1 - side) + tile, :, kind * HD : (kind + 1) * HD
                    ].astype(jnp.bfloat16)
                part(i, side, tile).start()
            return 0

        lax.fori_loop(0, devices, leave, 0)

        def both(peer):
            result(0, i, peer).start()
            result(1, i, peer).start()

        peers(both)
        result_local(0, i).start()
        result_local(1, i).start()
        return 0

    lax.fori_loop(0, heads, head_step, 0)

    def last(n, _):
        i = 1 + lax.div(n, devices)
        finish(i, lax.rem(n + 1, devices))
        return 0

    lax.fori_loop(0, (heads - 1) * devices, last, 0)

    def settle(i, _):
        for x in range(4):
            result_local(x, i).wait()
            whole(q_ref.at[i, others], out_send.at[i, x], out_recv.at[i, x]).wait()
            whole(q_ref.at[i, others], in_send.at[i, x], out_recv.at[i, x]).wait_send()
        for side in range(2):
            whole(
                kv_ref.at[i, pl.ds(TILES_DEV, TILES_DEV)], rim_send.at[i, side], rim_recv.at[i, side]
            ).wait_send()
            whole(low_ref.at[i], part_send.at[i, side], part_recv.at[i, side, 0]).wait_send()
        return 0

    lax.fori_loop(0, heads, settle, 0)


def fused(tile_list, tile_count, key, value, query, cotangent):
    heads = key.shape[1] // (TILES_DEV * HD)
    hbm = pl.BlockSpec(memory_space=pl.ANY)
    smem = pl.BlockSpec(memory_space=pltpu.SMEM)
    tokens = jax.ShapeDtypeStruct(key.shape, jnp.bfloat16)
    tiles = pltpu.VMEM((heads, TILES_DEV, TILE, HD), jnp.bfloat16)
    pairs = pltpu.VMEM((heads, TILES_DEV, 2, TILE, HD), jnp.bfloat16)
    dma = pltpu.SemaphoreType.DMA
    return pl.pallas_call(
        functools.partial(fused_kernel, heads),
        out_shape=(tokens,) * 4,
        in_specs=[smem, smem, hbm, hbm, hbm, hbm],
        out_specs=(hbm,) * 4,
        scratch_shapes=[
            pltpu.VMEM((heads, POOL, 2, TILE, HD), jnp.bfloat16),
            tiles,
            tiles,
            pltpu.VMEM((heads, POOL, TILE, 2 * HD), jnp.float32),
            pltpu.SMEM((TILES_DEV * POOL,), jnp.float32),
            pltpu.VMEM((2 * TILE, 2 * HD), jnp.bfloat16),
            pltpu.VMEM((FRAMES, 6 * TILE, TILE), jnp.float32),
            pltpu.VMEM((FRAMES, 6 * TILE, TILE), jnp.float32),
            pltpu.VMEM((FRAMES, 8, TILE), jnp.float32),
            pltpu.VMEM((HD, TILE), jnp.float32),
            pltpu.VMEM((HD, TILE), jnp.float32),
            tiles,
            tiles,
            tiles,
            tiles,
            pairs,
            pairs,
            pairs,
            pairs,
            dma((heads, 4)),
            dma((heads, 2, TILES_DEV)),
            dma((heads, 2)),
            dma((heads, 4)),
            dma((heads, 2)),
            dma((heads, 2)),
            dma((heads, 4)),
            dma((heads, 4)),
            dma((heads, 4)),
            dma((heads, 2, TILES_DEV)),
            dma((heads, 2)),
        ],
        compiler_params=pltpu.CompilerParams(
            collective_id=0, has_side_effects=True, vmem_limit_bytes=58 * 2**20
        ),
        name="fused",
    )(tile_list, tile_count, key, value, query, cotangent)


def per_device(query, key, value, grad_out, tile_list, tile_count):
    return tuple(fused(tile_list.T, tile_count, key, value, query, grad_out))


def solution(mesh):
    tokens = P(("seq", "head"), None)
    return jax.shard_map(
        per_device,
        mesh=mesh,
        in_specs=(tokens, tokens, tokens, tokens, P(), P()),
        out_specs=(tokens, tokens, tokens, tokens),
        check_vma=False,
    )
```

```python
import functools

import jax
import jax.numpy as jnp
from jax import lax
from jax.experimental import pallas as pl
from jax.experimental.pallas import tpu as pltpu
from jax.sharding import PartitionSpec as P

HD = 128
TILE = 128
TILES_DEV = 8
FRAMES = 3
POOL = FRAMES * TILES_DEV
LIST = 12
SCALING = HD ** (-0.5)
LOG2E = 1.4426950408889634
UNUSED = 1e30
MESH = pl.DeviceIdType.MESH


def swapped(head, flag):
    return head + flag * (1 - 2 * lax.rem(head, 2))


def placement():
    slabs = lax.axis_size("seq")
    slab, head = lax.axis_index("seq"), lax.axis_index("head")
    above, below = lax.rem(slab + 1, slabs), lax.rem(slab + slabs - 1, slabs)

    def flag(s):
        return lax.rem(lax.div(s, 2), 2)

    own = flag(slab)
    head_above = swapped(head, lax.rem(own + flag(above), 2))
    head_below = swapped(head, lax.rem(own + flag(below), 2))
    return slab, head, own, (above, head_above), (below, head_below)


def entry_barrier(slab, head, devices, neighbours):
    barrier = pltpu.get_barrier_semaphore()

    def greet(r, _):
        pl.semaphore_signal(
            barrier, inc=1, device_id={"seq": slab, "head": lax.rem(head + r, devices)}, device_id_type=MESH
        )
        return 0

    lax.fori_loop(1, devices, greet, 0)
    for s, h in neighbours:
        pl.semaphore_signal(barrier, inc=1, device_id={"seq": s, "head": h}, device_id_type=MESH)
    pl.semaphore_wait(barrier, devices - 1 + len(neighbours))


def folded(op, rows):
    return functools.reduce(op, [rows[r : r + 8] for r in range(0, rows.shape[0], 8)])


def fused_kernel(
    heads,
    list_ref, count_ref, k_hbm, v_hbm, q_hbm, g_hbm,
    o_out, dq_out, dk_out, dv_out,
    kv_ref, q_ref, g_ref, acc_ref, mask_ref, e_ref, dp_ref, stat_ref,
    o_ref, dq_ref, dk_ref, dv_ref, low_ref, up_ref, from_below, from_above,
    local_sem, kv_recv, qg_recv, in_send, rim_recv, rim_send,
    out_local, out_send, out_recv, part_recv, part_send,
):
    devices = lax.axis_size("head")
    slab, head, flag, above, below = placement()
    sources = (v_hbm, k_hbm, q_hbm, g_hbm)
    results = ((o_ref, o_out), (dq_ref, dq_out), (dk_ref, dk_out), (dv_ref, dv_out))

    def columns(group, i):
        return pl.ds(pl.multiple_of((group * heads + i) * HD, HD), HD)

    def landing(x, i, slot):
        return kv_ref.at[i, TILES_DEV + slot, x] if x < 2 else (q_ref, g_ref)[x - 2].at[i, slot]

    def local(x, i):
        return pltpu.make_async_copy(
            sources[x].at[:, columns(swapped(head, flag), i)], landing(x, i, head), local_sem.at[i, x]
        )

    def incoming(x, i, peer, slot):
        return pltpu.make_async_remote_copy(
            src_ref=sources[x].at[:, columns(swapped(peer, flag), i)],
            dst_ref=landing(x, i, slot),
            send_sem=in_send.at[i, x],
            recv_sem=kv_recv.at[i, x, slot] if x < 2 else qg_recv.at[i, x - 2],
            device_id={"seq": slab, "head": peer},
            device_id_type=MESH,
        )

    def whole(ref, send_sem, recv_sem):
        return pltpu.make_async_remote_copy(
            src_ref=ref, dst_ref=ref, send_sem=send_sem, recv_sem=recv_sem,
            device_id={"seq": above[0], "head": above[1]}, device_id_type=MESH,
        )

    def rim(i, side, tile):
        s, h = (above, below)[side]
        return pltpu.make_async_remote_copy(
            src_ref=kv_ref.at[i, TILES_DEV + tile],
            dst_ref=kv_ref.at[i, 2 * TILES_DEV * side + tile],
            send_sem=rim_send.at[i, side],
            recv_sem=rim_recv.at[i, side],
            device_id={"seq": s, "head": h},
            device_id_type=MESH,
        )

    def part(i, side, tile):
        s, h = (above, below)[side]
        return pltpu.make_async_remote_copy(
            src_ref=(up_ref, low_ref)[side].at[i, tile],
            dst_ref=(from_below, from_above)[side].at[i, tile],
            send_sem=part_send.at[i, side],
            recv_sem=part_recv.at[i, side, tile],
            device_id={"seq": s, "head": h},
            device_id_type=MESH,
        )

    def result_local(x, i):
        src, dst = results[x]
        return pltpu.make_async_copy(
            src.at[i, head], dst.at[:, columns(swapped(head, flag), i)], out_local.at[i, x]
        )

    def result(x, i, peer):
        src, dst = results[x]
        return pltpu.make_async_remote_copy(
            src_ref=src.at[i, peer],
            dst_ref=dst.at[:, columns(swapped(head, flag), i)],
            send_sem=out_send.at[i, x],
            recv_sem=out_recv.at[i, x],
            device_id={"seq": slab, "head": peer},
            device_id_type=MESH,
        )

    def peers(body):
        def step(r, _):
            body(lax.rem(head + r, devices))
            return 0

        lax.fori_loop(1, devices, step, 0)

    def send(i, streams):
        def both(peer):
            for x in streams:
                incoming(x, i, peer, head).start()

        peers(both)

    def forward(i, r):
        tile = lax.rem(head + r, devices)

        @pl.when(r == 0)
        def _():
            local(0, i).wait()
            local(1, i).wait()

        @pl.when(r > 0)
        def _():
            incoming(0, i, tile, tile).wait_recv()
            incoming(1, i, tile, tile).wait_recv()

        rim(i, 0, tile).start()
        rim(i, 1, tile).start()

    def finish(i, r):
        tile = lax.rem(head + r, devices)
        part(i, 0, tile).wait_recv()
        part(i, 1, tile).wait_recv()
        dv = acc_ref[i, 0, TILES_DEV + tile] + (
            from_below[i, tile, 0].astype(jnp.float32) + from_above[i, tile, 0].astype(jnp.float32)
        )
        dk = acc_ref[i, 1, TILES_DEV + tile] + (
            from_below[i, tile, 1].astype(jnp.float32) + from_above[i, tile, 1].astype(jnp.float32)
        )
        dk_ref[i, tile] = (SCALING * dk).astype(jnp.bfloat16)
        dv_ref[i, tile] = dv.astype(jnp.bfloat16)

        @pl.when(r > 0)
        def _():
            result(2, i, tile).start()
            result(3, i, tile).start()

        @pl.when(r == 0)
        def _():
            result_local(2, i).start()
            result_local(3, i).start()

    def attend(i, a, start, count):
        rows = count * TILE
        queries = q_ref[i, pl.ds(a, 2)].reshape(2 * TILE, HD)
        cotangents = g_ref[i, pl.ds(a, 2)].reshape(2 * TILE, HD)
        nt, nn, tn = ((((x,), (y,)), ((), ())) for x, y in ((1, 1), (1, 0), (0, 0)))
        dot = functools.partial(lax.dot_general, preferred_element_type=jnp.float32)
        slots = [(f, u, f * TILES_DEV + start + u) for f in range(FRAMES) for u in range(count)]

        def pairs(f):
            first = f * TILES_DEV + start
            values = kv_ref[i, pl.ds(first, count), 0].reshape(rows, HD)
            keys = kv_ref[i, pl.ds(first, count), 1].reshape(rows, HD)
            return values, keys

        def tile(u):
            return slice(u * TILE, (u + 1) * TILE)

        for f in range(FRAMES):
            values, keys = pairs(f)
            scores = dot(keys, queries, nt)
            grad_probs = dot(values, cotangents, nt)
            for u in range(count):
                n = f * count + u
                score, grad_prob = scores[tile(u)], grad_probs[tile(u)]
                top = jnp.max(folded(jnp.maximum, score), axis=0, keepdims=True)
                e = jnp.exp2((score - top) * (SCALING * LOG2E))
                e_ref[n] = e
                dp_ref[n] = grad_prob
                stat_ref[n, 0:1] = top
                stat_ref[n, 1:2] = jnp.sum(folded(jnp.add, e), axis=0, keepdims=True)
                stat_ref[n, 2:3] = jnp.sum(folded(jnp.add, e * grad_prob), axis=0, keepdims=True)

        left = lax.broadcasted_iota(jnp.int32, (1, 2 * TILE), 1) < TILE
        tops = [
            stat_ref[n, 0:1] - jnp.where(left, mask_ref[a * POOL + slot], mask_ref[(a + 1) * POOL + slot])
            for n, (_, _, slot) in enumerate(slots)
        ]
        top = functools.reduce(jnp.maximum, tops)
        weights = [jnp.exp2((t - top) * (SCALING * LOG2E)) for t in tops]
        total = sum(w * stat_ref[n, 1:2] for n, w in enumerate(weights))
        delta = sum(w * stat_ref[n, 2:3] for n, w in enumerate(weights)) / total
        inverse = 1.0 / total
        for n, weight in enumerate(weights):
            stat_ref[n, 3:4] = weight * inverse

        out = jnp.zeros((HD, 2 * TILE), jnp.float32)
        dq = jnp.zeros((HD, 2 * TILE), jnp.float32)
        for f in range(FRAMES):
            values, keys = pairs(f)
            probs, grad_scores = [], []
            for u in range(count):
                n = f * count + u
                p = e_ref[n] * stat_ref[n, 3:4]
                probs.append(p.astype(jnp.bfloat16))
                grad_scores.append((p * (dp_ref[n] - delta)).astype(jnp.bfloat16))
            pb = jnp.concatenate(probs, axis=0)
            ds = jnp.concatenate(grad_scores, axis=0)
            dv = dot(pb, cotangents, nn)
            dk = dot(ds, queries, nn)
            for u in range(count):
                slot = f * TILES_DEV + start + u
                acc_ref[i, 0, slot] += dv[tile(u)]
                acc_ref[i, 1, slot] += dk[tile(u)]
            out = out + dot(values, pb, tn)
            dq = dq + dot(keys, ds, tn)
        o_ref[i, pl.ds(a, 2)] = out.T.astype(jnp.bfloat16).reshape(2, TILE, HD)
        dq_ref[i, pl.ds(a, 2)] = (dq.T * SCALING).astype(jnp.bfloat16).reshape(2, TILE, HD)

    for i in range(heads):
        for x in range(4):
            local(x, i).start()
    entry_barrier(slab, head, devices, (above, below))
    send(0, (0, 1))
    forward(0, 0)
    send(0, (2, 3))

    def masks(a, _):
        used = count_ref[slab * TILES_DEV + a]
        listed = [
            jnp.where(j < used, list_ref[j, slab * TILES_DEV + a] - (slab - 1) * TILES_DEV, -1)
            for j in range(LIST)
        ]

        def one(slot, _):
            hit = functools.reduce(jnp.logical_or, [entry == slot for entry in listed])
            mask_ref[a * POOL + slot] = jnp.where(hit, 0.0, UNUSED).astype(jnp.float32)
            return 0

        lax.fori_loop(0, POOL, one, 0)
        return 0

    lax.fori_loop(0, TILES_DEV, masks, 0)

    def first_tiles(r, _):
        forward(0, r)
        return 0

    lax.fori_loop(1, devices, first_tiles, 0)
    send(1, (0, 1))

    others = pl.ds(0, devices - 1)

    def head_step(i, _):
        def clear(slot, _):
            for kind in range(2):
                acc_ref[i, kind, slot] = jnp.zeros((TILE, HD), jnp.float32)
            return 0

        lax.fori_loop(0, POOL, clear, 0)

        @pl.when(i < heads - 1)
        def _():
            send(i + 1, (2, 3))

        @pl.when(i < heads - 2)
        def _():
            send(i + 2, (0, 1))

        def ahead(r, _):
            @pl.when(i < heads - 1)
            def _():
                forward(i + 1, r)

            @pl.when(i == heads - 1)
            def _():
                finish(0, lax.rem(r + 1, devices))

            return 0

        lax.fori_loop(0, devices, ahead, 0)
        for x in (2, 3):
            local(x, i).wait()
            whole(q_ref.at[i, others], in_send.at[i, x], qg_recv.at[i, x - 2]).wait_recv()
        for side in range(2):
            whole(
                kv_ref.at[i, pl.ds(TILES_DEV, TILES_DEV)], rim_send.at[i, side], rim_recv.at[i, side]
            ).wait_recv()

        def outer(n, _):
            attend(i, 6 * n, 4 * n, 4)
            return 0

        def inner(n, _):
            attend(i, 2 * n + 2, 2 * n, 6)
            return 0

        lax.fori_loop(0, 2, outer, 0)
        lax.fori_loop(0, 2, inner, 0)

        def leave(r, _):
            for side, (ref, (_, h)) in enumerate(((up_ref, above), (low_ref, below))):
                tile = lax.rem(h + 1 + r, devices)
                for kind in range(2):
                    slot = 2 * TILES_DEV * (1 - side) + tile
                    ref[i, tile, kind] = acc_ref[i, kind, slot].astype(jnp.bfloat16)
                part(i, side, tile).start()
            return 0

        lax.fori_loop(0, devices, leave, 0)

        def both(peer):
            result(0, i, peer).start()
            result(1, i, peer).start()

        peers(both)
        result_local(0, i).start()
        result_local(1, i).start()
        return 0

    lax.fori_loop(0, heads, head_step, 0)

    def last(n, _):
        i = 1 + lax.div(n, devices)
        finish(i, lax.rem(n + 1, devices))
        return 0

    lax.fori_loop(0, (heads - 1) * devices, last, 0)

    def settle(i, _):
        for x in range(4):
            result_local(x, i).wait()
            whole(q_ref.at[i, others], out_send.at[i, x], out_recv.at[i, x]).wait()
            whole(q_ref.at[i, others], in_send.at[i, x], out_recv.at[i, x]).wait_send()
        for side in range(2):
            whole(
                kv_ref.at[i, pl.ds(TILES_DEV, TILES_DEV)], rim_send.at[i, side], rim_recv.at[i, side]
            ).wait_send()
            whole(low_ref.at[i], part_send.at[i, side], part_recv.at[i, side, 0]).wait_send()
        return 0

    lax.fori_loop(0, heads, settle, 0)


def fused(tile_list, tile_count, key, value, query, cotangent):
    heads = key.shape[1] // (TILES_DEV * HD)
    hbm = pl.BlockSpec(memory_space=pl.ANY)
    smem = pl.BlockSpec(memory_space=pltpu.SMEM)
    tokens = jax.ShapeDtypeStruct(key.shape, jnp.bfloat16)
    tiles = pltpu.VMEM((heads, TILES_DEV, TILE, HD), jnp.bfloat16)
    pairs = pltpu.VMEM((heads, TILES_DEV, 2, TILE, HD), jnp.bfloat16)
    dma = pltpu.SemaphoreType.DMA
    return pl.pallas_call(
        functools.partial(fused_kernel, heads),
        out_shape=(tokens,) * 4,
        in_specs=[smem, smem, hbm, hbm, hbm, hbm],
        out_specs=(hbm,) * 4,
        scratch_shapes=[
            pltpu.VMEM((heads, POOL, 2, TILE, HD), jnp.bfloat16),
            tiles,
            tiles,
            pltpu.VMEM((heads, 2, POOL, TILE, HD), jnp.float32),
            pltpu.SMEM((TILES_DEV * POOL,), jnp.float32),
            pltpu.VMEM((6 * FRAMES, TILE, 2 * TILE), jnp.float32),
            pltpu.VMEM((6 * FRAMES, TILE, 2 * TILE), jnp.float32),
            pltpu.VMEM((6 * FRAMES, 8, 2 * TILE), jnp.float32),
            tiles,
            tiles,
            tiles,
            tiles,
            pairs,
            pairs,
            pairs,
            pairs,
            dma((heads, 4)),
            dma((heads, 2, TILES_DEV)),
            dma((heads, 2)),
            dma((heads, 4)),
            dma((heads, 2)),
            dma((heads, 2)),
            dma((heads, 4)),
            dma((heads, 4)),
            dma((heads, 4)),
            dma((heads, 2, TILES_DEV)),
            dma((heads, 2)),
        ],
        compiler_params=pltpu.CompilerParams(
            collective_id=0, has_side_effects=True, vmem_limit_bytes=58 * 2**20
        ),
        name="fused",
    )(tile_list, tile_count, key, value, query, cotangent)


def emit_kernel(*refs):
    count = len(refs) // 2
    for n in range(count):
        refs[count + n][...] = refs[n][...]


def emit(arrays):
    rows, columns = arrays[0].shape
    spec = pl.BlockSpec((rows // 8, columns), lambda n: (n, 0))
    return pl.pallas_call(
        emit_kernel,
        grid=(8,),
        out_shape=tuple(jax.ShapeDtypeStruct(a.shape, a.dtype) for a in arrays),
        in_specs=[spec] * len(arrays),
        out_specs=(spec,) * len(arrays),
        name="emit",
    )(*arrays)


def per_device(query, key, value, grad_out, tile_list, tile_count):
    return tuple(emit(fused(tile_list.T, tile_count, key, value, query, grad_out)))


def solution(mesh):
    tokens = P(("seq", "head"), None)
    return jax.shard_map(
        per_device,
        mesh=mesh,
        in_specs=(tokens, tokens, tokens, tokens, P(), P()),
        out_specs=(tokens, tokens, tokens, tokens),
        check_vma=False,
    )
```

```python
import functools

import jax
import jax.numpy as jnp
from jax import lax
from jax.experimental import pallas as pl
from jax.experimental.pallas import tpu as pltpu
from jax.sharding import PartitionSpec as P

HD = 128
TILE = 128
TILES_DEV = 8
FRAMES = 3
POOL = FRAMES * TILES_DEV
LIST = 12
SCALING = HD ** (-0.5)
LOG2E = 1.4426950408889634
UNUSED = 1e30
MESH = pl.DeviceIdType.MESH


def swapped(head, flag):
    return head + flag * (1 - 2 * lax.rem(head, 2))


def placement():
    slabs = lax.axis_size("seq")
    slab, head = lax.axis_index("seq"), lax.axis_index("head")
    above, below = lax.rem(slab + 1, slabs), lax.rem(slab + slabs - 1, slabs)

    def flag(s):
        return lax.rem(lax.div(s, 2), 2)

    own = flag(slab)
    head_above = swapped(head, lax.rem(own + flag(above), 2))
    head_below = swapped(head, lax.rem(own + flag(below), 2))
    return slab, head, own, (above, head_above), (below, head_below)


def entry_barrier(slab, head, devices, neighbours):
    barrier = pltpu.get_barrier_semaphore()

    def greet(r, _):
        pl.semaphore_signal(
            barrier, inc=1, device_id={"seq": slab, "head": lax.rem(head + r, devices)}, device_id_type=MESH
        )
        return 0

    lax.fori_loop(1, devices, greet, 0)
    for s, h in neighbours:
        pl.semaphore_signal(barrier, inc=1, device_id={"seq": s, "head": h}, device_id_type=MESH)
    pl.semaphore_wait(barrier, devices - 1 + len(neighbours))


def folded(op, rows):
    return functools.reduce(op, [rows[r : r + 8] for r in range(0, rows.shape[0], 8)])


def fused_kernel(
    heads,
    list_ref, count_ref, k_hbm, v_hbm, q_hbm, g_hbm,
    o_out, dq_out, dk_out, dv_out,
    kv_ref, q_ref, g_ref, acc_ref, mask_ref, e_ref, dp_ref, stat_ref,
    o_ref, dq_ref, dk_ref, dv_ref, low_ref, up_ref, from_below, from_above,
    local_sem, kv_recv, qg_recv, in_send, rim_recv, rim_send,
    out_local, out_send, out_recv, part_recv, part_send,
):
    devices = lax.axis_size("head")
    slab, head, flag, above, below = placement()
    sources = (v_hbm, k_hbm, q_hbm, g_hbm)
    results = ((o_ref, o_out), (dq_ref, dq_out), (dk_ref, dk_out), (dv_ref, dv_out))

    def columns(group, i):
        return pl.ds(pl.multiple_of((group * heads + i) * HD, HD), HD)

    def landing(x, i, slot):
        return kv_ref.at[i, TILES_DEV + slot, x] if x < 2 else (q_ref, g_ref)[x - 2].at[i, slot]

    def local(x, i):
        return pltpu.make_async_copy(
            sources[x].at[:, columns(swapped(head, flag), i)], landing(x, i, head), local_sem.at[i, x]
        )

    def incoming(x, i, peer, slot):
        return pltpu.make_async_remote_copy(
            src_ref=sources[x].at[:, columns(swapped(peer, flag), i)],
            dst_ref=landing(x, i, slot),
            send_sem=in_send.at[i, x],
            recv_sem=kv_recv.at[i, x, slot] if x < 2 else qg_recv.at[i, x - 2],
            device_id={"seq": slab, "head": peer},
            device_id_type=MESH,
        )

    def whole(ref, send_sem, recv_sem):
        return pltpu.make_async_remote_copy(
            src_ref=ref, dst_ref=ref, send_sem=send_sem, recv_sem=recv_sem,
            device_id={"seq": above[0], "head": above[1]}, device_id_type=MESH,
        )

    def rim(i, side, tile):
        s, h = (above, below)[side]
        return pltpu.make_async_remote_copy(
            src_ref=kv_ref.at[i, TILES_DEV + tile],
            dst_ref=kv_ref.at[i, 2 * TILES_DEV * side + tile],
            send_sem=rim_send.at[i, side],
            recv_sem=rim_recv.at[i, side],
            device_id={"seq": s, "head": h},
            device_id_type=MESH,
        )

    def part(i, side, tile):
        s, h = (above, below)[side]
        return pltpu.make_async_remote_copy(
            src_ref=(up_ref, low_ref)[side].at[i, tile],
            dst_ref=(from_below, from_above)[side].at[i, tile],
            send_sem=part_send.at[i, side],
            recv_sem=part_recv.at[i, side, tile],
            device_id={"seq": s, "head": h},
            device_id_type=MESH,
        )

    def result_local(x, i):
        src, dst = results[x]
        return pltpu.make_async_copy(
            src.at[i, head], dst.at[:, columns(swapped(head, flag), i)], out_local.at[i, x]
        )

    def result(x, i, peer):
        src, dst = results[x]
        return pltpu.make_async_remote_copy(
            src_ref=src.at[i, peer],
            dst_ref=dst.at[:, columns(swapped(head, flag), i)],
            send_sem=out_send.at[i, x],
            recv_sem=out_recv.at[i, x],
            device_id={"seq": slab, "head": peer},
            device_id_type=MESH,
        )

    def peers(body):
        def step(r, _):
            body(lax.rem(head + r, devices))
            return 0

        lax.fori_loop(1, devices, step, 0)

    def send(i, streams):
        def both(peer):
            for x in streams:
                incoming(x, i, peer, head).start()

        peers(both)

    def pass_on(i, tile):
        rim(i, 0, tile).start()
        rim(i, 1, tile).start()

    def forward_own(i):
        local(0, i).wait()
        local(1, i).wait()
        pass_on(i, head)

    def forward(i):
        def arrived(peer):
            incoming(0, i, peer, peer).wait_recv()
            incoming(1, i, peer, peer).wait_recv()
            pass_on(i, peer)

        peers(arrived)

    def forward_halves():
        for x in range(2):

            def arrived(peer):
                incoming(x, 0, peer, peer).wait_recv()
                for side, (s, h) in enumerate((above, below)):
                    pltpu.make_async_remote_copy(
                        src_ref=kv_ref.at[0, TILES_DEV + peer, x],
                        dst_ref=kv_ref.at[0, 2 * TILES_DEV * side + peer, x],
                        send_sem=rim_send.at[0, side],
                        recv_sem=rim_recv.at[0, side],
                        device_id={"seq": s, "head": h},
                        device_id_type=MESH,
                    ).start()

            peers(arrived)

    def finish(i, r):
        tile = lax.rem(head + r, devices)
        part(i, 0, tile).wait_recv()
        part(i, 1, tile).wait_recv()
        dv = acc_ref[i, 0, TILES_DEV + tile] + (
            from_below[i, tile, 0].astype(jnp.float32) + from_above[i, tile, 0].astype(jnp.float32)
        )
        dk = acc_ref[i, 1, TILES_DEV + tile] + (
            from_below[i, tile, 1].astype(jnp.float32) + from_above[i, tile, 1].astype(jnp.float32)
        )
        dk_ref[i, tile] = (SCALING * dk).astype(jnp.bfloat16)
        dv_ref[i, tile] = dv.astype(jnp.bfloat16)

        @pl.when(r > 0)
        def _():
            result(2, i, tile).start()
            result(3, i, tile).start()

        @pl.when(r == 0)
        def _():
            result_local(2, i).start()
            result_local(3, i).start()

    def attend(i, a, start, count):
        rows = count * TILE
        queries = q_ref[i, pl.ds(a, 2)].reshape(2 * TILE, HD)
        cotangents = g_ref[i, pl.ds(a, 2)].reshape(2 * TILE, HD)
        nt, nn, tn = ((((x,), (y,)), ((), ())) for x, y in ((1, 1), (1, 0), (0, 0)))
        dot = functools.partial(lax.dot_general, preferred_element_type=jnp.float32)
        slots = [(f, u, f * TILES_DEV + start + u) for f in range(FRAMES) for u in range(count)]

        def pairs(f):
            first = f * TILES_DEV + start
            values = kv_ref[i, pl.ds(first, count), 0].reshape(rows, HD)
            keys = kv_ref[i, pl.ds(first, count), 1].reshape(rows, HD)
            return values, keys

        def tile(u):
            return slice(u * TILE, (u + 1) * TILE)

        for f in range(FRAMES):
            values, keys = pairs(f)
            scores = dot(keys, queries, nt)
            grad_probs = dot(values, cotangents, nt)
            for u in range(count):
                n = f * count + u
                score, grad_prob = scores[tile(u)], grad_probs[tile(u)]
                top = jnp.max(folded(jnp.maximum, score), axis=0, keepdims=True)
                e = jnp.exp2((score - top) * (SCALING * LOG2E))
                e_ref[n] = e
                dp_ref[n] = grad_prob
                stat_ref[n, 0:1] = top
                stat_ref[n, 1:2] = jnp.sum(folded(jnp.add, e), axis=0, keepdims=True)
                stat_ref[n, 2:3] = jnp.sum(folded(jnp.add, e * grad_prob), axis=0, keepdims=True)

        left = lax.broadcasted_iota(jnp.int32, (1, 2 * TILE), 1) < TILE
        tops = [
            stat_ref[n, 0:1] - jnp.where(left, mask_ref[a * POOL + slot], mask_ref[(a + 1) * POOL + slot])
            for n, (_, _, slot) in enumerate(slots)
        ]
        top = functools.reduce(jnp.maximum, tops)
        weights = [jnp.exp2((t - top) * (SCALING * LOG2E)) for t in tops]
        total = sum(w * stat_ref[n, 1:2] for n, w in enumerate(weights))
        delta = sum(w * stat_ref[n, 2:3] for n, w in enumerate(weights)) / total
        inverse = 1.0 / total
        for n, weight in enumerate(weights):
            stat_ref[n, 3:4] = weight * inverse

        out = jnp.zeros((HD, 2 * TILE), jnp.float32)
        dq = jnp.zeros((HD, 2 * TILE), jnp.float32)
        for f in range(FRAMES):
            values, keys = pairs(f)
            probs, grad_scores = [], []
            for u in range(count):
                n = f * count + u
                p = e_ref[n] * stat_ref[n, 3:4]
                probs.append(p.astype(jnp.bfloat16))
                grad_scores.append((p * (dp_ref[n] - delta)).astype(jnp.bfloat16))
            pb = jnp.concatenate(probs, axis=0)
            ds = jnp.concatenate(grad_scores, axis=0)
            dv = dot(pb, cotangents, nn)
            dk = dot(ds, queries, nn)
            for u in range(count):
                slot = f * TILES_DEV + start + u
                acc_ref[i, 0, slot] += dv[tile(u)]
                acc_ref[i, 1, slot] += dk[tile(u)]
            out = out + dot(values, pb, tn)
            dq = dq + dot(keys, ds, tn)
        o_ref[i, pl.ds(a, 2)] = out.T.astype(jnp.bfloat16).reshape(2, TILE, HD)
        dq_ref[i, pl.ds(a, 2)] = (dq.T * SCALING).astype(jnp.bfloat16).reshape(2, TILE, HD)

    for i in range(heads):
        for x in range(4):
            local(x, i).start()
    entry_barrier(slab, head, devices, (above, below))
    send(0, (0,))
    send(0, (1,))
    for i in range(heads):
        forward_own(i)
    for i in range(1, heads):
        send(i, (0, 1))
    for i in range(heads):
        send(i, (2, 3))

    def masks(a, _):
        used = count_ref[slab * TILES_DEV + a]
        listed = [
            jnp.where(j < used, list_ref[j, slab * TILES_DEV + a] - (slab - 1) * TILES_DEV, -1)
            for j in range(LIST)
        ]

        def one(slot, _):
            hit = functools.reduce(jnp.logical_or, [entry == slot for entry in listed])
            mask_ref[a * POOL + slot] = jnp.where(hit, 0.0, UNUSED).astype(jnp.float32)
            return 0

        lax.fori_loop(0, POOL, one, 0)
        return 0

    lax.fori_loop(0, TILES_DEV, masks, 0)

    forward_halves()
    for i in range(1, heads):
        forward(i)

    others = pl.ds(0, devices - 1)

    def leave(i):
        def parts(r, _):
            for side, (ref, (_, h)) in enumerate(((up_ref, above), (low_ref, below))):
                tile = lax.rem(h + 1 + r, devices)
                slot = 2 * TILES_DEV * (1 - side) + tile
                for kind in range(2):
                    ref[i, tile, kind] = acc_ref[i, kind, slot].astype(jnp.bfloat16)
                part(i, side, tile).start()
            return 0

        lax.fori_loop(0, devices, parts, 0)

        def both(peer):
            result(0, i, peer).start()
            result(1, i, peer).start()

        peers(both)
        result_local(0, i).start()
        result_local(1, i).start()

    def head_step(i, _):
        @pl.when(i > 0)
        def _():
            leave(i - 1)

        def clear(slot, _):
            for kind in range(2):
                acc_ref[i, kind, slot] = jnp.zeros((TILE, HD), jnp.float32)
            return 0

        lax.fori_loop(0, POOL, clear, 0)

        for x in (2, 3):
            local(x, i).wait()
            whole(q_ref.at[i, others], in_send.at[i, x], qg_recv.at[i, x - 2]).wait_recv()
        for side in range(2):
            whole(
                kv_ref.at[i, pl.ds(TILES_DEV, TILES_DEV)], rim_send.at[i, side], rim_recv.at[i, side]
            ).wait_recv()

        def outer(n, _):
            attend(i, 6 * n, 4 * n, 4)
            return 0

        def inner(n, _):
            attend(i, 2 * n + 2, 2 * n, 6)
            return 0

        lax.fori_loop(0, 2, outer, 0)
        lax.fori_loop(0, 2, inner, 0)
        return 0

    lax.fori_loop(0, heads, head_step, 0)
    leave(heads - 1)

    def last(n, _):
        finish(lax.div(n, devices), lax.rem(n + 1, devices))
        return 0

    lax.fori_loop(0, heads * devices, last, 0)

    def settle(i, _):
        for x in range(4):
            result_local(x, i).wait()
            whole(q_ref.at[i, others], out_send.at[i, x], out_recv.at[i, x]).wait()
            whole(q_ref.at[i, others], in_send.at[i, x], out_recv.at[i, x]).wait_send()
        for side in range(2):
            whole(
                kv_ref.at[i, pl.ds(TILES_DEV, TILES_DEV)], rim_send.at[i, side], rim_recv.at[i, side]
            ).wait_send()
            whole(low_ref.at[i], part_send.at[i, side], part_recv.at[i, side, 0]).wait_send()
        return 0

    lax.fori_loop(0, heads, settle, 0)


def fused(tile_list, tile_count, key, value, query, cotangent):
    heads = key.shape[1] // (TILES_DEV * HD)
    hbm = pl.BlockSpec(memory_space=pl.ANY)
    smem = pl.BlockSpec(memory_space=pltpu.SMEM)
    tokens = jax.ShapeDtypeStruct(key.shape, jnp.bfloat16)
    tiles = pltpu.VMEM((heads, TILES_DEV, TILE, HD), jnp.bfloat16)
    pairs = pltpu.VMEM((heads, TILES_DEV, 2, TILE, HD), jnp.bfloat16)
    dma = pltpu.SemaphoreType.DMA
    return pl.pallas_call(
        functools.partial(fused_kernel, heads),
        out_shape=(pltpu.VMEM(key.shape, jnp.bfloat16),) * 4,
        in_specs=[smem, smem, hbm, hbm, hbm, hbm],
        out_specs=(hbm,) * 4,
        scratch_shapes=[
            pltpu.VMEM((heads, POOL, 2, TILE, HD), jnp.bfloat16),
            tiles,
            tiles,
            pltpu.VMEM((heads, 2, POOL, TILE, HD), jnp.float32),
            pltpu.SMEM((TILES_DEV * POOL,), jnp.float32),
            pltpu.VMEM((6 * FRAMES, TILE, 2 * TILE), jnp.float32),
            pltpu.VMEM((6 * FRAMES, TILE, 2 * TILE), jnp.float32),
            pltpu.VMEM((6 * FRAMES, 8, 2 * TILE), jnp.float32),
            tiles,
            tiles,
            tiles,
            tiles,
            pairs,
            pairs,
            pairs,
            pairs,
            dma((heads, 4)),
            dma((heads, 2, TILES_DEV)),
            dma((heads, 2)),
            dma((heads, 4)),
            dma((heads, 2)),
            dma((heads, 2)),
            dma((heads, 4)),
            dma((heads, 4)),
            dma((heads, 4)),
            dma((heads, 2, TILES_DEV)),
            dma((heads, 2)),
        ],
        compiler_params=pltpu.CompilerParams(
            collective_id=0, has_side_effects=True, vmem_limit_bytes=36 * 2**20
        ),
        name="fused",
    )(tile_list, tile_count, key, value, query, cotangent)


def emit_kernel(*refs):
    count = len(refs) // 2
    sem = refs[-1]
    stores = [pltpu.make_async_copy(refs[n], refs[count + n], sem.at[n]) for n in range(count)]
    for store in stores:
        store.start()
    for store in stores:
        store.wait()


def emit(arrays):
    hbm = pl.BlockSpec(memory_space=pl.ANY)
    arrays = [pltpu.with_memory_space_constraint(a, pltpu.VMEM) for a in arrays]
    return pl.pallas_call(
        emit_kernel,
        out_shape=tuple(pltpu.HBM(a.shape, a.dtype) for a in arrays),
        in_specs=[hbm] * len(arrays),
        out_specs=(hbm,) * len(arrays),
        scratch_shapes=[pltpu.SemaphoreType.DMA((len(arrays),))],
        name="emit",
    )(*arrays)


def per_device(query, key, value, grad_out, tile_list, tile_count):
    tile_list, tile_count, query, key, value, grad_out = (
        pltpu.with_memory_space_constraint(x, pltpu.HBM)
        for x in (tile_list.T, tile_count, query, key, value, grad_out)
    )
    return tuple(emit(fused(tile_list, tile_count, key, value, query, grad_out)))


def solution(mesh):
    tokens = P(("seq", "head"), None)
    return jax.shard_map(
        per_device,
        mesh=mesh,
        in_specs=(tokens, tokens, tokens, tokens, P(), P()),
        out_specs=(tokens, tokens, tokens, tokens),
        check_vma=False,
    )
```

```python
import functools

import jax
import jax.numpy as jnp
from jax import lax
from jax.experimental import pallas as pl
from jax.experimental.pallas import tpu as pltpu
from jax.sharding import PartitionSpec as P

HD = 128
TILE = 128
TILES_DEV = 8
FRAMES = 3
POOL = FRAMES * TILES_DEV
LIST = 12
SCALING = HD ** (-0.5)
LOG2E = 1.4426950408889634
UNUSED = 1e30
MESH = pl.DeviceIdType.MESH


def swapped(head, flag):
    return head + flag * (1 - 2 * lax.rem(head, 2))


def placement():
    slabs = lax.axis_size("seq")
    slab, head = lax.axis_index("seq"), lax.axis_index("head")
    above, below = lax.rem(slab + 1, slabs), lax.rem(slab + slabs - 1, slabs)

    def flag(s):
        return lax.rem(lax.div(s, 2), 2)

    own = flag(slab)
    head_above = swapped(head, lax.rem(own + flag(above), 2))
    head_below = swapped(head, lax.rem(own + flag(below), 2))
    return slab, head, own, (above, head_above), (below, head_below)


def greet_all(slab, head, devices, neighbours):
    barrier = pltpu.get_barrier_semaphore()

    def greet(r, _):
        pl.semaphore_signal(
            barrier, inc=1, device_id={"seq": slab, "head": lax.rem(head + r, devices)}, device_id_type=MESH
        )
        return 0

    lax.fori_loop(1, devices, greet, 0)
    for s, h in neighbours:
        pl.semaphore_signal(barrier, inc=1, device_id={"seq": s, "head": h}, device_id_type=MESH)
    return barrier, devices - 1 + len(neighbours)


def folded(op, rows):
    return functools.reduce(op, [rows[r : r + 8] for r in range(0, rows.shape[0], 8)])


def fused_kernel(
    heads,
    list_ref, count_ref, k_hbm, v_hbm, q_hbm, g_hbm,
    o_out, dq_out, dk_out, dv_out,
    kv_ref, q_ref, g_ref, acc_ref, mask_ref, e_ref, dp_ref, stat_ref,
    o_ref, dq_ref, dk_ref, dv_ref, low_ref, up_ref, from_below, from_above,
    local_sem, kv_recv, qg_recv, in_send, rim_recv, rim_send,
    out_local, out_send, out_recv, part_recv, part_send,
):
    devices = lax.axis_size("head")
    slab, head, flag, above, below = placement()
    sources = (v_hbm, k_hbm, q_hbm, g_hbm)
    results = ((o_ref, o_out), (dq_ref, dq_out), (dk_ref, dk_out), (dv_ref, dv_out))

    def columns(group, i):
        return pl.ds(pl.multiple_of((group * heads + i) * HD, HD), HD)

    def landing(x, i, slot):
        return kv_ref.at[i, TILES_DEV + slot, x] if x < 2 else (q_ref, g_ref)[x - 2].at[i, slot]

    def local(x, i):
        return pltpu.make_async_copy(
            sources[x].at[:, columns(swapped(head, flag), i)], landing(x, i, head), local_sem.at[i, x]
        )

    def incoming(x, i, peer, slot):
        return pltpu.make_async_remote_copy(
            src_ref=sources[x].at[:, columns(swapped(peer, flag), i)],
            dst_ref=landing(x, i, slot),
            send_sem=in_send.at[i, x],
            recv_sem=kv_recv.at[i, x, slot] if x < 2 else qg_recv.at[i, x - 2],
            device_id={"seq": slab, "head": peer},
            device_id_type=MESH,
        )

    def whole(ref, send_sem, recv_sem):
        return pltpu.make_async_remote_copy(
            src_ref=ref, dst_ref=ref, send_sem=send_sem, recv_sem=recv_sem,
            device_id={"seq": above[0], "head": above[1]}, device_id_type=MESH,
        )

    def rim(i, side, tile):
        s, h = (above, below)[side]
        return pltpu.make_async_remote_copy(
            src_ref=kv_ref.at[i, TILES_DEV + tile],
            dst_ref=kv_ref.at[i, 2 * TILES_DEV * side + tile],
            send_sem=rim_send.at[i, side],
            recv_sem=rim_recv.at[i, side],
            device_id={"seq": s, "head": h},
            device_id_type=MESH,
        )

    def part(i, side, tile):
        s, h = (above, below)[side]
        return pltpu.make_async_remote_copy(
            src_ref=(up_ref, low_ref)[side].at[i, tile],
            dst_ref=(from_below, from_above)[side].at[i, tile],
            send_sem=part_send.at[i, side],
            recv_sem=part_recv.at[i, side, tile],
            device_id={"seq": s, "head": h},
            device_id_type=MESH,
        )

    def result_local(x, i):
        src, dst = results[x]
        return pltpu.make_async_copy(
            src.at[i, head], dst.at[:, columns(swapped(head, flag), i)], out_local.at[i, x]
        )

    def result(x, i, peer):
        src, dst = results[x]
        return pltpu.make_async_remote_copy(
            src_ref=src.at[i, peer],
            dst_ref=dst.at[:, columns(swapped(head, flag), i)],
            send_sem=out_send.at[i, x],
            recv_sem=out_recv.at[i, x],
            device_id={"seq": slab, "head": peer},
            device_id_type=MESH,
        )

    def peers(body):
        def step(r, _):
            body(lax.rem(head + r, devices))
            return 0

        lax.fori_loop(1, devices, step, 0)

    def send(i, streams):
        def both(peer):
            for x in streams:
                incoming(x, i, peer, head).start()

        peers(both)

    def pass_on(i, tile):
        rim(i, 0, tile).start()
        rim(i, 1, tile).start()

    def forward_own(i):
        local(0, i).wait()
        local(1, i).wait()
        pass_on(i, head)

    def forward(i):
        def arrived(peer):
            incoming(0, i, peer, peer).wait_recv()
            incoming(1, i, peer, peer).wait_recv()
            pass_on(i, peer)

        peers(arrived)

    def forward_halves():
        for x in range(2):

            def arrived(peer):
                incoming(x, 0, peer, peer).wait_recv()
                for side, (s, h) in enumerate((above, below)):
                    pltpu.make_async_remote_copy(
                        src_ref=kv_ref.at[0, TILES_DEV + peer, x],
                        dst_ref=kv_ref.at[0, 2 * TILES_DEV * side + peer, x],
                        send_sem=rim_send.at[0, side],
                        recv_sem=rim_recv.at[0, side],
                        device_id={"seq": s, "head": h},
                        device_id_type=MESH,
                    ).start()

            peers(arrived)

    def finish(i, r):
        tile = lax.rem(head + r, devices)
        part(i, 0, tile).wait_recv()
        part(i, 1, tile).wait_recv()
        dv = acc_ref[i, 0, TILES_DEV + tile] + (
            from_below[i, tile, 0].astype(jnp.float32) + from_above[i, tile, 0].astype(jnp.float32)
        )
        dk = acc_ref[i, 1, TILES_DEV + tile] + (
            from_below[i, tile, 1].astype(jnp.float32) + from_above[i, tile, 1].astype(jnp.float32)
        )
        dk_ref[i, tile] = (SCALING * dk).astype(jnp.bfloat16)
        dv_ref[i, tile] = dv.astype(jnp.bfloat16)

        @pl.when(r > 0)
        def _():
            result(2, i, tile).start()
            result(3, i, tile).start()

        @pl.when(r == 0)
        def _():
            result_local(2, i).start()
            result_local(3, i).start()

    def attend(i, a, start, count):
        rows = count * TILE
        queries = q_ref[i, pl.ds(a, 2)].reshape(2 * TILE, HD)
        cotangents = g_ref[i, pl.ds(a, 2)].reshape(2 * TILE, HD)
        nt, nn, tn = ((((x,), (y,)), ((), ())) for x, y in ((1, 1), (1, 0), (0, 0)))
        dot = functools.partial(lax.dot_general, preferred_element_type=jnp.float32)
        slots = [(f, u, f * TILES_DEV + start + u) for f in range(FRAMES) for u in range(count)]

        def pairs(f):
            first = f * TILES_DEV + start
            values = kv_ref[i, pl.ds(first, count), 0].reshape(rows, HD)
            keys = kv_ref[i, pl.ds(first, count), 1].reshape(rows, HD)
            return values, keys

        def tile(u):
            return slice(u * TILE, (u + 1) * TILE)

        for f in range(FRAMES):
            values, keys = pairs(f)
            scores = dot(keys, queries, nt)
            grad_probs = dot(values, cotangents, nt)
            for u in range(count):
                n = f * count + u
                score, grad_prob = scores[tile(u)], grad_probs[tile(u)]
                top = jnp.max(folded(jnp.maximum, score), axis=0, keepdims=True)
                e = jnp.exp2((score - top) * (SCALING * LOG2E))
                e_ref[n] = e
                dp_ref[n] = grad_prob
                stat_ref[n, 0:1] = top
                stat_ref[n, 1:2] = jnp.sum(folded(jnp.add, e), axis=0, keepdims=True)
                stat_ref[n, 2:3] = jnp.sum(folded(jnp.add, e * grad_prob), axis=0, keepdims=True)

        left = lax.broadcasted_iota(jnp.int32, (1, 2 * TILE), 1) < TILE
        tops = [
            stat_ref[n, 0:1] - jnp.where(left, mask_ref[a * POOL + slot], mask_ref[(a + 1) * POOL + slot])
            for n, (_, _, slot) in enumerate(slots)
        ]
        top = functools.reduce(jnp.maximum, tops)
        weights = [jnp.exp2((t - top) * (SCALING * LOG2E)) for t in tops]
        total = sum(w * stat_ref[n, 1:2] for n, w in enumerate(weights))
        delta = sum(w * stat_ref[n, 2:3] for n, w in enumerate(weights)) / total
        inverse = 1.0 / total
        for n, weight in enumerate(weights):
            stat_ref[n, 3:4] = weight * inverse

        out = jnp.zeros((HD, 2 * TILE), jnp.float32)
        dq = jnp.zeros((HD, 2 * TILE), jnp.float32)
        for f in range(FRAMES):
            values, keys = pairs(f)
            probs, grad_scores = [], []
            for u in range(count):
                n = f * count + u
                p = e_ref[n] * stat_ref[n, 3:4]
                probs.append(p.astype(jnp.bfloat16))
                grad_scores.append((p * (dp_ref[n] - delta)).astype(jnp.bfloat16))
            pb = jnp.concatenate(probs, axis=0)
            ds = jnp.concatenate(grad_scores, axis=0)
            dv = dot(pb, cotangents, nn)
            dk = dot(ds, queries, nn)
            for u in range(count):
                slot = f * TILES_DEV + start + u
                acc_ref[i, 0, slot] += dv[tile(u)]
                acc_ref[i, 1, slot] += dk[tile(u)]
            out = out + dot(values, pb, tn)
            dq = dq + dot(keys, ds, tn)
        o_ref[i, pl.ds(a, 2)] = out.T.astype(jnp.bfloat16).reshape(2, TILE, HD)
        dq_ref[i, pl.ds(a, 2)] = (dq.T * SCALING).astype(jnp.bfloat16).reshape(2, TILE, HD)

    barrier, greetings = greet_all(slab, head, devices, (above, below))
    for x in range(4):
        for i in range(heads):
            local(x, i).start()
    pl.semaphore_wait(barrier, greetings)
    send(0, (0,))
    send(0, (1,))
    for i in range(heads):
        forward_own(i)
    for i in range(1, heads):
        send(i, (0, 1))
    for i in range(heads):
        send(i, (2, 3))

    def masks(a, _):
        used = count_ref[slab * TILES_DEV + a]
        listed = [
            jnp.where(j < used, list_ref[j, slab * TILES_DEV + a] - (slab - 1) * TILES_DEV, -1)
            for j in range(LIST)
        ]

        def one(slot, _):
            hit = functools.reduce(jnp.logical_or, [entry == slot for entry in listed])
            mask_ref[a * POOL + slot] = jnp.where(hit, 0.0, UNUSED).astype(jnp.float32)
            return 0

        lax.fori_loop(0, POOL, one, 0)
        return 0

    lax.fori_loop(0, TILES_DEV, masks, 0)

    forward_halves()
    for i in range(1, heads):
        forward(i)

    others = pl.ds(0, devices - 1)

    def leave(i):
        def parts(r, _):
            for side, (ref, (_, h)) in enumerate(((up_ref, above), (low_ref, below))):
                tile = lax.rem(h + 1 + r, devices)
                slot = 2 * TILES_DEV * (1 - side) + tile
                for kind in range(2):
                    ref[i, tile, kind] = acc_ref[i, kind, slot].astype(jnp.bfloat16)
                part(i, side, tile).start()
            return 0

        lax.fori_loop(0, devices, parts, 0)

        def both(peer):
            result(0, i, peer).start()
            result(1, i, peer).start()

        peers(both)
        result_local(0, i).start()
        result_local(1, i).start()

    def head_step(i, _):
        @pl.when(i > 0)
        def _():
            leave(i - 1)

        def clear(slot, _):
            for kind in range(2):
                acc_ref[i, kind, slot] = jnp.zeros((TILE, HD), jnp.float32)
            return 0

        lax.fori_loop(0, POOL, clear, 0)

        for x in (2, 3):
            local(x, i).wait()
            whole(q_ref.at[i, others], in_send.at[i, x], qg_recv.at[i, x - 2]).wait_recv()
        for side in range(2):
            whole(
                kv_ref.at[i, pl.ds(TILES_DEV, TILES_DEV)], rim_send.at[i, side], rim_recv.at[i, side]
            ).wait_recv()

        def first_finish(r):
            @pl.when(i == heads - 1)
            def _():
                finish(0, lax.rem(r + 1, devices))
                finish(0, lax.rem(r + 2, devices))

        def outer(n, _):
            attend(i, 6 * n, 4 * n, 4)
            first_finish(2 * n)
            return 0

        def inner(n, _):
            attend(i, 2 * n + 2, 2 * n, 6)
            first_finish(2 * n + 4)
            return 0

        lax.fori_loop(0, 2, outer, 0)
        lax.fori_loop(0, 2, inner, 0)
        return 0

    lax.fori_loop(0, heads, head_step, 0)
    leave(heads - 1)

    def settle_arrivals(i, _):
        for x in range(4):
            whole(q_ref.at[i, others], in_send.at[i, x], out_recv.at[i, x]).wait_send()
        for side in range(2):
            whole(
                kv_ref.at[i, pl.ds(TILES_DEV, TILES_DEV)], rim_send.at[i, side], rim_recv.at[i, side]
            ).wait_send()
        return 0

    lax.fori_loop(0, heads, settle_arrivals, 0)

    def last(n, _):
        finish(1 + lax.div(n, devices), lax.rem(n + 1, devices))
        return 0

    lax.fori_loop(0, (heads - 1) * devices, last, 0)

    def settle_results(i, _):
        for x in range(4):
            result_local(x, i).wait()
            whole(q_ref.at[i, others], out_send.at[i, x], out_recv.at[i, x]).wait()
        for side in range(2):
            whole(low_ref.at[i], part_send.at[i, side], part_recv.at[i, side, 0]).wait_send()
        return 0

    lax.fori_loop(0, heads, settle_results, 0)


def fused(tile_list, tile_count, key, value, query, cotangent):
    heads = key.shape[1] // (TILES_DEV * HD)
    hbm = pl.BlockSpec(memory_space=pl.ANY)
    smem = pl.BlockSpec(memory_space=pltpu.SMEM)
    tokens = jax.ShapeDtypeStruct(key.shape, jnp.bfloat16)
    tiles = pltpu.VMEM((heads, TILES_DEV, TILE, HD), jnp.bfloat16)
    pairs = pltpu.VMEM((heads, TILES_DEV, 2, TILE, HD), jnp.bfloat16)
    dma = pltpu.SemaphoreType.DMA
    return pl.pallas_call(
        functools.partial(fused_kernel, heads),
        out_shape=(pltpu.VMEM(key.shape, jnp.bfloat16),) * 4,
        in_specs=[smem, smem, hbm, hbm, hbm, hbm],
        out_specs=(hbm,) * 4,
        scratch_shapes=[
            pltpu.VMEM((heads, POOL, 2, TILE, HD), jnp.bfloat16),
            tiles,
            tiles,
            pltpu.VMEM((heads, 2, POOL, TILE, HD), jnp.float32),
            pltpu.SMEM((TILES_DEV * POOL,), jnp.float32),
            pltpu.VMEM((6 * FRAMES, TILE, 2 * TILE), jnp.float32),
            pltpu.VMEM((6 * FRAMES, TILE, 2 * TILE), jnp.float32),
            pltpu.VMEM((6 * FRAMES, 8, 2 * TILE), jnp.float32),
            tiles,
            tiles,
            tiles,
            tiles,
            pairs,
            pairs,
            pairs,
            pairs,
            dma((heads, 4)),
            dma((heads, 2, TILES_DEV)),
            dma((heads, 2)),
            dma((heads, 4)),
            dma((heads, 2)),
            dma((heads, 2)),
            dma((heads, 4)),
            dma((heads, 4)),
            dma((heads, 4)),
            dma((heads, 2, TILES_DEV)),
            dma((heads, 2)),
        ],
        compiler_params=pltpu.CompilerParams(
            collective_id=0, has_side_effects=True, vmem_limit_bytes=36 * 2**20
        ),
        name="fused",
    )(tile_list, tile_count, key, value, query, cotangent)


def emit_kernel(*refs):
    count = len(refs) // 2
    sem = refs[-1]
    stores = [pltpu.make_async_copy(refs[n], refs[count + n], sem.at[n]) for n in range(count)]
    for store in stores:
        store.start()
    for store in stores:
        store.wait()


def emit(arrays):
    hbm = pl.BlockSpec(memory_space=pl.ANY)
    arrays = [pltpu.with_memory_space_constraint(a, pltpu.VMEM) for a in arrays]
    return pl.pallas_call(
        emit_kernel,
        out_shape=tuple(pltpu.HBM(a.shape, a.dtype) for a in arrays),
        in_specs=[hbm] * len(arrays),
        out_specs=(hbm,) * len(arrays),
        scratch_shapes=[pltpu.SemaphoreType.DMA((len(arrays),))],
        name="emit",
    )(*arrays)


def per_device(query, key, value, grad_out, tile_list, tile_count):
    tile_list, tile_count, query, key, value, grad_out = (
        pltpu.with_memory_space_constraint(x, pltpu.HBM)
        for x in (tile_list.T, tile_count, query, key, value, grad_out)
    )
    return tuple(emit(fused(tile_list, tile_count, key, value, query, grad_out)))


def solution(mesh):
    tokens = P(("seq", "head"), None)
    return jax.shard_map(
        per_device,
        mesh=mesh,
        in_specs=(tokens, tokens, tokens, tokens, P(), P()),
        out_specs=(tokens, tokens, tokens, tokens),
        check_vma=False,
    )
```

```python
import functools

import jax
import jax.numpy as jnp
from jax import lax
from jax.experimental import pallas as pl
from jax.experimental.pallas import tpu as pltpu
from jax.sharding import PartitionSpec as P

HD = 128
TILE = 128
TILES_DEV = 8
FRAMES = 3
POOL = FRAMES * TILES_DEV
LIST = 12
SCALING = HD ** (-0.5)
LOG2E = 1.4426950408889634
UNUSED = 1e30
MESH = pl.DeviceIdType.MESH


def swapped(head, flag):
    return head + flag * (1 - 2 * lax.rem(head, 2))


def placement():
    slabs = lax.axis_size("seq")
    slab, head = lax.axis_index("seq"), lax.axis_index("head")
    above, below = lax.rem(slab + 1, slabs), lax.rem(slab + slabs - 1, slabs)

    def flag(s):
        return lax.rem(lax.div(s, 2), 2)

    own = flag(slab)
    head_above = swapped(head, lax.rem(own + flag(above), 2))
    head_below = swapped(head, lax.rem(own + flag(below), 2))
    return slab, head, own, (above, head_above), (below, head_below)


def greet_all(slab, head, devices, neighbours):
    barrier = pltpu.get_barrier_semaphore()

    def greet(r, _):
        pl.semaphore_signal(
            barrier, inc=1, device_id={"seq": slab, "head": lax.rem(head + r, devices)}, device_id_type=MESH
        )
        return 0

    lax.fori_loop(1, devices, greet, 0)
    for s, h in neighbours:
        pl.semaphore_signal(barrier, inc=1, device_id={"seq": s, "head": h}, device_id_type=MESH)
    return barrier, devices - 1 + len(neighbours)


def folded(op, rows):
    return functools.reduce(op, [rows[r : r + 8] for r in range(0, rows.shape[0], 8)])


def fused_kernel(
    heads,
    list_hbm, count_hbm, k_hbm, v_hbm, q_hbm, g_hbm,
    o_out, dq_out, dk_out, dv_out,
    list_ref, count_ref, table_sem, kv_ref, q_ref, g_ref, acc_ref, mask_ref, e_ref, dp_ref, stat_ref,
    o_ref, dq_ref, dk_ref, dv_ref, low_ref, up_ref, from_below, from_above,
    local_sem, kv_recv, qg_recv, in_send, rim_recv, rim_send,
    out_local, out_send, out_recv, part_recv, part_send,
):
    devices = lax.axis_size("head")
    slab, head, flag, above, below = placement()
    sources = (v_hbm, k_hbm, q_hbm, g_hbm)
    results = ((o_ref, o_out), (dq_ref, dq_out), (dk_ref, dk_out), (dv_ref, dv_out))

    def columns(group, i):
        return pl.ds(pl.multiple_of((group * heads + i) * HD, HD), HD)

    def landing(x, i, slot):
        return kv_ref.at[i, TILES_DEV + slot, x] if x < 2 else (q_ref, g_ref)[x - 2].at[i, slot]

    def local(x, i):
        return pltpu.make_async_copy(
            sources[x].at[:, columns(swapped(head, flag), i)], landing(x, i, head), local_sem.at[i, x]
        )

    def incoming(x, i, peer, slot):
        return pltpu.make_async_remote_copy(
            src_ref=sources[x].at[:, columns(swapped(peer, flag), i)],
            dst_ref=landing(x, i, slot),
            send_sem=in_send.at[i, x],
            recv_sem=kv_recv.at[i, x, slot] if x < 2 else qg_recv.at[i, x - 2],
            device_id={"seq": slab, "head": peer},
            device_id_type=MESH,
        )

    def whole(ref, send_sem, recv_sem):
        return pltpu.make_async_remote_copy(
            src_ref=ref, dst_ref=ref, send_sem=send_sem, recv_sem=recv_sem,
            device_id={"seq": above[0], "head": above[1]}, device_id_type=MESH,
        )

    def rim(i, side, tile):
        s, h = (above, below)[side]
        return pltpu.make_async_remote_copy(
            src_ref=kv_ref.at[i, TILES_DEV + tile],
            dst_ref=kv_ref.at[i, 2 * TILES_DEV * side + tile],
            send_sem=rim_send.at[i, side],
            recv_sem=rim_recv.at[i, side],
            device_id={"seq": s, "head": h},
            device_id_type=MESH,
        )

    def part(i, side, tile):
        s, h = (above, below)[side]
        return pltpu.make_async_remote_copy(
            src_ref=(up_ref, low_ref)[side].at[i, tile],
            dst_ref=(from_below, from_above)[side].at[i, tile],
            send_sem=part_send.at[i, side],
            recv_sem=part_recv.at[i, side, tile],
            device_id={"seq": s, "head": h},
            device_id_type=MESH,
        )

    def result_local(x, i):
        src, dst = results[x]
        return pltpu.make_async_copy(
            src.at[i, head], dst.at[:, columns(swapped(head, flag), i)], out_local.at[i, x]
        )

    def result(x, i, peer):
        src, dst = results[x]
        return pltpu.make_async_remote_copy(
            src_ref=src.at[i, peer],
            dst_ref=dst.at[:, columns(swapped(head, flag), i)],
            send_sem=out_send.at[i, x],
            recv_sem=out_recv.at[i, x],
            device_id={"seq": slab, "head": peer},
            device_id_type=MESH,
        )

    def peers(body):
        def step(r, _):
            body(lax.rem(head + r, devices))
            return 0

        lax.fori_loop(1, devices, step, 0)

    def send(i, streams):
        def both(peer):
            for x in streams:
                incoming(x, i, peer, head).start()

        peers(both)

    def pass_on(i, tile):
        rim(i, 0, tile).start()
        rim(i, 1, tile).start()

    def forward_own(i):
        local(0, i).wait()
        local(1, i).wait()
        pass_on(i, head)

    def forward(i):
        def arrived(peer):
            incoming(0, i, peer, peer).wait_recv()
            incoming(1, i, peer, peer).wait_recv()
            pass_on(i, peer)

        peers(arrived)

    def forward_halves():
        for x in range(2):

            def arrived(peer):
                incoming(x, 0, peer, peer).wait_recv()
                for side, (s, h) in enumerate((above, below)):
                    pltpu.make_async_remote_copy(
                        src_ref=kv_ref.at[0, TILES_DEV + peer, x],
                        dst_ref=kv_ref.at[0, 2 * TILES_DEV * side + peer, x],
                        send_sem=rim_send.at[0, side],
                        recv_sem=rim_recv.at[0, side],
                        device_id={"seq": s, "head": h},
                        device_id_type=MESH,
                    ).start()

            peers(arrived)

    def finish(i, r):
        tile = lax.rem(head + r, devices)
        part(i, 0, tile).wait_recv()
        part(i, 1, tile).wait_recv()
        dv = acc_ref[i, 0, TILES_DEV + tile] + (
            from_below[i, tile, 0].astype(jnp.float32) + from_above[i, tile, 0].astype(jnp.float32)
        )
        dk = acc_ref[i, 1, TILES_DEV + tile] + (
            from_below[i, tile, 1].astype(jnp.float32) + from_above[i, tile, 1].astype(jnp.float32)
        )
        dk_ref[i, tile] = (SCALING * dk).astype(jnp.bfloat16)
        dv_ref[i, tile] = dv.astype(jnp.bfloat16)

        @pl.when(r > 0)
        def _():
            result(2, i, tile).start()
            result(3, i, tile).start()

        @pl.when(r == 0)
        def _():
            result_local(2, i).start()
            result_local(3, i).start()

    def attend(i, a, start, count):
        rows = count * TILE
        queries = q_ref[i, pl.ds(a, 2)].reshape(2 * TILE, HD)
        cotangents = g_ref[i, pl.ds(a, 2)].reshape(2 * TILE, HD)
        nt, nn, tn = ((((x,), (y,)), ((), ())) for x, y in ((1, 1), (1, 0), (0, 0)))
        dot = functools.partial(lax.dot_general, preferred_element_type=jnp.float32)
        slots = [(f, u, f * TILES_DEV + start + u) for f in range(FRAMES) for u in range(count)]

        def pairs(f):
            first = f * TILES_DEV + start
            values = kv_ref[i, pl.ds(first, count), 0].reshape(rows, HD)
            keys = kv_ref[i, pl.ds(first, count), 1].reshape(rows, HD)
            return values, keys

        def tile(u):
            return slice(u * TILE, (u + 1) * TILE)

        for f in range(FRAMES):
            values, keys = pairs(f)
            scores = dot(keys, queries, nt)
            grad_probs = dot(values, cotangents, nt)
            for u in range(count):
                n = f * count + u
                score, grad_prob = scores[tile(u)], grad_probs[tile(u)]
                top = jnp.max(folded(jnp.maximum, score), axis=0, keepdims=True)
                e = jnp.exp2((score - top) * (SCALING * LOG2E))
                e_ref[n] = e
                dp_ref[n] = grad_prob
                stat_ref[n, 0:1] = top
                stat_ref[n, 1:2] = jnp.sum(folded(jnp.add, e), axis=0, keepdims=True)
                stat_ref[n, 2:3] = jnp.sum(folded(jnp.add, e * grad_prob), axis=0, keepdims=True)

        left = lax.broadcasted_iota(jnp.int32, (1, 2 * TILE), 1) < TILE
        tops = [
            stat_ref[n, 0:1] - jnp.where(left, mask_ref[a * POOL + slot], mask_ref[(a + 1) * POOL + slot])
            for n, (_, _, slot) in enumerate(slots)
        ]
        top = functools.reduce(jnp.maximum, tops)
        weights = [jnp.exp2((t - top) * (SCALING * LOG2E)) for t in tops]
        total = sum(w * stat_ref[n, 1:2] for n, w in enumerate(weights))
        delta = sum(w * stat_ref[n, 2:3] for n, w in enumerate(weights)) / total
        inverse = 1.0 / total
        for n, weight in enumerate(weights):
            stat_ref[n, 3:4] = weight * inverse

        out = jnp.zeros((HD, 2 * TILE), jnp.float32)
        dq = jnp.zeros((HD, 2 * TILE), jnp.float32)
        for f in range(FRAMES):
            values, keys = pairs(f)
            probs, grad_scores = [], []
            for u in range(count):
                n = f * count + u
                p = e_ref[n] * stat_ref[n, 3:4]
                probs.append(p.astype(jnp.bfloat16))
                grad_scores.append((p * (dp_ref[n] - delta)).astype(jnp.bfloat16))
            pb = jnp.concatenate(probs, axis=0)
            ds = jnp.concatenate(grad_scores, axis=0)
            dv = dot(pb, cotangents, nn)
            dk = dot(ds, queries, nn)
            for u in range(count):
                slot = f * TILES_DEV + start + u
                acc_ref[i, 0, slot] += dv[tile(u)]
                acc_ref[i, 1, slot] += dk[tile(u)]
            out = out + dot(values, pb, tn)
            dq = dq + dot(keys, ds, tn)
        o_ref[i, pl.ds(a, 2)] = out.T.astype(jnp.bfloat16).reshape(2, TILE, HD)
        dq_ref[i, pl.ds(a, 2)] = (dq.T * SCALING).astype(jnp.bfloat16).reshape(2, TILE, HD)

    barrier, greetings = greet_all(slab, head, devices, (above, below))
    for x in range(4):
        for i in range(heads):
            local(x, i).start()
    tables = [
        pltpu.make_async_copy(list_hbm, list_ref, table_sem.at[0]),
        pltpu.make_async_copy(count_hbm, count_ref, table_sem.at[1]),
    ]
    for table in tables:
        table.start()
    pl.semaphore_wait(barrier, greetings)
    send(0, (0,))
    send(0, (1,))
    for i in range(heads):
        forward_own(i)
    for i in range(1, heads):
        send(i, (0, 1))
    for i in range(heads):
        send(i, (2, 3))

    for table in tables:
        table.wait()

    def masks(a, _):
        used = count_ref[slab * TILES_DEV + a]
        listed = [
            jnp.where(j < used, list_ref[j, slab * TILES_DEV + a] - (slab - 1) * TILES_DEV, -1)
            for j in range(LIST)
        ]

        def one(slot, _):
            hit = functools.reduce(jnp.logical_or, [entry == slot for entry in listed])
            mask_ref[a * POOL + slot] = jnp.where(hit, 0.0, UNUSED).astype(jnp.float32)
            return 0

        lax.fori_loop(0, POOL, one, 0)
        return 0

    lax.fori_loop(0, TILES_DEV, masks, 0)

    forward_halves()
    for i in range(1, heads):
        forward(i)

    others = pl.ds(0, devices - 1)

    def leave(i):
        def parts(r, _):
            for side, (ref, (_, h)) in enumerate(((up_ref, above), (low_ref, below))):
                tile = lax.rem(h + 1 + r, devices)
                slot = 2 * TILES_DEV * (1 - side) + tile
                for kind in range(2):
                    ref[i, tile, kind] = acc_ref[i, kind, slot].astype(jnp.bfloat16)
                part(i, side, tile).start()
            return 0

        lax.fori_loop(0, devices, parts, 0)

        def both(peer):
            result(0, i, peer).start()
            result(1, i, peer).start()

        peers(both)
        result_local(0, i).start()
        result_local(1, i).start()

    def head_step(i, _):
        @pl.when(i > 0)
        def _():
            leave(i - 1)

        def clear(slot, _):
            for kind in range(2):
                acc_ref[i, kind, slot] = jnp.zeros((TILE, HD), jnp.float32)
            return 0

        lax.fori_loop(0, POOL, clear, 0)

        for x in (2, 3):
            local(x, i).wait()
            whole(q_ref.at[i, others], in_send.at[i, x], qg_recv.at[i, x - 2]).wait_recv()
        for side in range(2):
            whole(
                kv_ref.at[i, pl.ds(TILES_DEV, TILES_DEV)], rim_send.at[i, side], rim_recv.at[i, side]
            ).wait_recv()

        def first_finish(r):
            @pl.when(i == heads - 1)
            def _():
                finish(0, lax.rem(r + 1, devices))
                finish(0, lax.rem(r + 2, devices))

        def outer(n, _):
            attend(i, 6 * n, 4 * n, 4)
            first_finish(2 * n)
            return 0

        def inner(n, _):
            attend(i, 2 * n + 2, 2 * n, 6)
            first_finish(2 * n + 4)
            return 0

        lax.fori_loop(0, 2, outer, 0)
        lax.fori_loop(0, 2, inner, 0)
        return 0

    lax.fori_loop(0, heads, head_step, 0)
    leave(heads - 1)

    def settle_arrivals(i, _):
        for x in range(4):
            whole(q_ref.at[i, others], in_send.at[i, x], out_recv.at[i, x]).wait_send()
        for side in range(2):
            whole(
                kv_ref.at[i, pl.ds(TILES_DEV, TILES_DEV)], rim_send.at[i, side], rim_recv.at[i, side]
            ).wait_send()
        return 0

    lax.fori_loop(0, heads, settle_arrivals, 0)

    def last(n, _):
        finish(1 + lax.div(n, devices), lax.rem(n + 1, devices))
        return 0

    lax.fori_loop(0, (heads - 1) * devices, last, 0)

    def settle_results(i, _):
        for x in range(4):
            result_local(x, i).wait()
            whole(q_ref.at[i, others], out_send.at[i, x], out_recv.at[i, x]).wait()
        for side in range(2):
            whole(low_ref.at[i], part_send.at[i, side], part_recv.at[i, side, 0]).wait_send()
        return 0

    lax.fori_loop(0, heads, settle_results, 0)


def fused(tile_list, tile_count, key, value, query, cotangent):
    heads = key.shape[1] // (TILES_DEV * HD)
    hbm = pl.BlockSpec(memory_space=pl.ANY)
    tokens = jax.ShapeDtypeStruct(key.shape, jnp.bfloat16)
    tiles = pltpu.VMEM((heads, TILES_DEV, TILE, HD), jnp.bfloat16)
    pairs = pltpu.VMEM((heads, TILES_DEV, 2, TILE, HD), jnp.bfloat16)
    dma = pltpu.SemaphoreType.DMA
    return pl.pallas_call(
        functools.partial(fused_kernel, heads),
        out_shape=(pltpu.VMEM(key.shape, jnp.bfloat16),) * 4,
        in_specs=[hbm] * 6,
        out_specs=(hbm,) * 4,
        scratch_shapes=[
            pltpu.SMEM(tile_list.shape, jnp.int32),
            pltpu.SMEM(tile_count.shape, jnp.int32),
            dma((2,)),
            pltpu.VMEM((heads, POOL, 2, TILE, HD), jnp.bfloat16),
            tiles,
            tiles,
            pltpu.VMEM((heads, 2, POOL, TILE, HD), jnp.float32),
            pltpu.SMEM((TILES_DEV * POOL,), jnp.float32),
            pltpu.VMEM((6 * FRAMES, TILE, 2 * TILE), jnp.float32),
            pltpu.VMEM((6 * FRAMES, TILE, 2 * TILE), jnp.float32),
            pltpu.VMEM((6 * FRAMES, 8, 2 * TILE), jnp.float32),
            tiles,
            tiles,
            tiles,
            tiles,
            pairs,
            pairs,
            pairs,
            pairs,
            dma((heads, 4)),
            dma((heads, 2, TILES_DEV)),
            dma((heads, 2)),
            dma((heads, 4)),
            dma((heads, 2)),
            dma((heads, 2)),
            dma((heads, 4)),
            dma((heads, 4)),
            dma((heads, 4)),
            dma((heads, 2, TILES_DEV)),
            dma((heads, 2)),
        ],
        compiler_params=pltpu.CompilerParams(
            collective_id=0, has_side_effects=True, vmem_limit_bytes=36 * 2**20
        ),
        name="fused",
    )(tile_list, tile_count, key, value, query, cotangent)


def emit_kernel(*refs):
    count = len(refs) // 2
    sem = refs[-1]
    stores = [pltpu.make_async_copy(refs[n], refs[count + n], sem.at[n]) for n in range(count)]
    for store in stores:
        store.start()
    for store in stores:
        store.wait()


def emit(arrays):
    hbm = pl.BlockSpec(memory_space=pl.ANY)
    arrays = [pltpu.with_memory_space_constraint(a, pltpu.VMEM) for a in arrays]
    return pl.pallas_call(
        emit_kernel,
        out_shape=tuple(pltpu.HBM(a.shape, a.dtype) for a in arrays),
        in_specs=[hbm] * len(arrays),
        out_specs=(hbm,) * len(arrays),
        scratch_shapes=[pltpu.SemaphoreType.DMA((len(arrays),))],
        name="emit",
    )(*arrays)


def per_device(query, key, value, grad_out, tile_list, tile_count):
    tile_list, tile_count, query, key, value, grad_out = (
        pltpu.with_memory_space_constraint(x, pltpu.HBM)
        for x in (tile_list.T, tile_count, query, key, value, grad_out)
    )
    return tuple(emit(fused(tile_list, tile_count, key, value, query, grad_out)))


def solution(mesh):
    tokens = P(("seq", "head"), None)
    return jax.shard_map(
        per_device,
        mesh=mesh,
        in_specs=(tokens, tokens, tokens, tokens, P(), P()),
        out_specs=(tokens, tokens, tokens, tokens),
        check_vma=False,
    )
```

```python
import functools

import jax
import jax.numpy as jnp
from jax import lax
from jax.experimental import pallas as pl
from jax.experimental.pallas import tpu as pltpu
from jax.sharding import PartitionSpec as P

HD = 128
TILE = 128
TILES_DEV = 8
FRAMES = 3
POOL = FRAMES * TILES_DEV
LIST = 12
SCALING = HD ** (-0.5)
LOG2E = 1.4426950408889634
UNUSED = 1e30
MESH = pl.DeviceIdType.MESH


def swapped(head, flag):
    return head + flag * (1 - 2 * lax.rem(head, 2))


def placement():
    slabs = lax.axis_size("seq")
    slab, head = lax.axis_index("seq"), lax.axis_index("head")
    above, below = lax.rem(slab + 1, slabs), lax.rem(slab + slabs - 1, slabs)

    def flag(s):
        return lax.rem(lax.div(s, 2), 2)

    own = flag(slab)
    head_above = swapped(head, lax.rem(own + flag(above), 2))
    head_below = swapped(head, lax.rem(own + flag(below), 2))
    return slab, head, own, (above, head_above), (below, head_below)


def greet_all(slab, head, devices, neighbours):
    barrier = pltpu.get_barrier_semaphore()

    def greet(r, _):
        pl.semaphore_signal(
            barrier, inc=1, device_id={"seq": slab, "head": lax.rem(head + r, devices)}, device_id_type=MESH
        )
        return 0

    lax.fori_loop(1, devices, greet, 0)
    for s, h in neighbours:
        pl.semaphore_signal(barrier, inc=1, device_id={"seq": s, "head": h}, device_id_type=MESH)
    return barrier, devices - 1 + len(neighbours)


def folded(op, rows):
    return functools.reduce(op, [rows[r : r + 8] for r in range(0, rows.shape[0], 8)])


def fused_kernel(
    heads,
    list_hbm, count_hbm, k_hbm, v_hbm, q_hbm, g_hbm,
    o_out, dq_out, dk_out, dv_out,
    list_ref, count_ref, table_sem, kv_ref, q_ref, g_ref, acc_ref, mask_ref, e_ref, dp_ref, stat_ref,
    o_ref, dq_ref, dk_ref, dv_ref, low_ref, up_ref, from_below, from_above,
    local_sem, kv_recv, qg_recv, in_send, rim_recv, rim_send,
    out_local, out_send, out_recv, part_recv, part_send,
):
    devices = lax.axis_size("head")
    slab, head, flag, above, below = placement()
    sources = (v_hbm, k_hbm, q_hbm, g_hbm)
    results = ((o_ref, o_out), (dq_ref, dq_out), (dk_ref, dk_out), (dv_ref, dv_out))

    def columns(group, i):
        return pl.ds(pl.multiple_of((group * heads + i) * HD, HD), HD)

    def landing(x, i, slot):
        return kv_ref.at[i, TILES_DEV + slot, x] if x < 2 else (q_ref, g_ref)[x - 2].at[i, slot]

    def local(x, i):
        return pltpu.make_async_copy(
            sources[x].at[:, columns(swapped(head, flag), i)], landing(x, i, head), local_sem.at[i, x]
        )

    def incoming(x, i, peer, slot):
        return pltpu.make_async_remote_copy(
            src_ref=sources[x].at[:, columns(swapped(peer, flag), i)],
            dst_ref=landing(x, i, slot),
            send_sem=in_send.at[i, x],
            recv_sem=kv_recv.at[i, x, slot] if x < 2 else qg_recv.at[i, x - 2],
            device_id={"seq": slab, "head": peer},
            device_id_type=MESH,
        )

    def whole(ref, send_sem, recv_sem):
        return pltpu.make_async_remote_copy(
            src_ref=ref, dst_ref=ref, send_sem=send_sem, recv_sem=recv_sem,
            device_id={"seq": above[0], "head": above[1]}, device_id_type=MESH,
        )

    def rim(i, side, tile):
        s, h = (above, below)[side]
        return pltpu.make_async_remote_copy(
            src_ref=kv_ref.at[i, TILES_DEV + tile],
            dst_ref=kv_ref.at[i, 2 * TILES_DEV * side + tile],
            send_sem=rim_send.at[i, side],
            recv_sem=rim_recv.at[i, side],
            device_id={"seq": s, "head": h},
            device_id_type=MESH,
        )

    def part(i, side, tile):
        s, h = (above, below)[side]
        return pltpu.make_async_remote_copy(
            src_ref=(up_ref, low_ref)[side].at[i, tile],
            dst_ref=(from_below, from_above)[side].at[i, tile],
            send_sem=part_send.at[i, side],
            recv_sem=part_recv.at[i, side, tile],
            device_id={"seq": s, "head": h},
            device_id_type=MESH,
        )

    def result_local(x, i):
        src, dst = results[x]
        return pltpu.make_async_copy(
            src.at[i, head], dst.at[:, columns(swapped(head, flag), i)], out_local.at[i, x]
        )

    def result(x, i, peer):
        src, dst = results[x]
        return pltpu.make_async_remote_copy(
            src_ref=src.at[i, peer],
            dst_ref=dst.at[:, columns(swapped(head, flag), i)],
            send_sem=out_send.at[i, x],
            recv_sem=out_recv.at[i, x],
            device_id={"seq": slab, "head": peer},
            device_id_type=MESH,
        )

    def peers(body):
        def step(r, _):
            body(lax.rem(head + r, devices))
            return 0

        lax.fori_loop(1, devices, step, 0)

    def send(i, streams):
        def both(peer):
            for x in streams:
                incoming(x, i, peer, head).start()

        peers(both)

    def pass_on(i, tile):
        rim(i, 0, tile).start()
        rim(i, 1, tile).start()

    def forward_own(i):
        local(0, i).wait()
        local(1, i).wait()
        pass_on(i, head)

    def forward(i):
        def arrived(peer):
            incoming(0, i, peer, peer).wait_recv()
            incoming(1, i, peer, peer).wait_recv()
            pass_on(i, peer)

        peers(arrived)

    def forward_halves():
        for x in range(2):

            def arrived(peer):
                incoming(x, 0, peer, peer).wait_recv()
                for side, (s, h) in enumerate((above, below)):
                    pltpu.make_async_remote_copy(
                        src_ref=kv_ref.at[0, TILES_DEV + peer, x],
                        dst_ref=kv_ref.at[0, 2 * TILES_DEV * side + peer, x],
                        send_sem=rim_send.at[0, side],
                        recv_sem=rim_recv.at[0, side],
                        device_id={"seq": s, "head": h},
                        device_id_type=MESH,
                    ).start()

            peers(arrived)

    def finish(i, r):
        tile = lax.rem(head + r, devices)
        part(i, 0, tile).wait_recv()
        part(i, 1, tile).wait_recv()
        dv = acc_ref[i, 0, TILES_DEV + tile] + (
            from_below[i, tile, 0].astype(jnp.float32) + from_above[i, tile, 0].astype(jnp.float32)
        )
        dk = acc_ref[i, 1, TILES_DEV + tile] + (
            from_below[i, tile, 1].astype(jnp.float32) + from_above[i, tile, 1].astype(jnp.float32)
        )
        dk_ref[i, tile] = (SCALING * dk).astype(jnp.bfloat16)
        dv_ref[i, tile] = dv.astype(jnp.bfloat16)

        @pl.when(r > 0)
        def _():
            result(2, i, tile).start()
            result(3, i, tile).start()

        @pl.when(r == 0)
        def _():
            result_local(2, i).start()
            result_local(3, i).start()

    def attend(i, a, start, count):
        rows = count * TILE
        queries = q_ref[i, pl.ds(a, 2)].reshape(2 * TILE, HD)
        cotangents = g_ref[i, pl.ds(a, 2)].reshape(2 * TILE, HD)
        nt, nn, tn = ((((x,), (y,)), ((), ())) for x, y in ((1, 1), (1, 0), (0, 0)))
        dot = functools.partial(lax.dot_general, preferred_element_type=jnp.float32)
        slots = [(f, u, f * TILES_DEV + start + u) for f in range(FRAMES) for u in range(count)]

        def pairs(f):
            first = f * TILES_DEV + start
            values = kv_ref[i, pl.ds(first, count), 0].reshape(rows, HD)
            keys = kv_ref[i, pl.ds(first, count), 1].reshape(rows, HD)
            return values, keys

        def tile(u):
            return slice(u * TILE, (u + 1) * TILE)

        for f in range(FRAMES):
            values, keys = pairs(f)
            scores = dot(keys, queries, nt)
            grad_probs = dot(values, cotangents, nt)
            for u in range(count):
                n = f * count + u
                score, grad_prob = scores[tile(u)], grad_probs[tile(u)]
                top = jnp.max(folded(jnp.maximum, score), axis=0, keepdims=True)
                e = jnp.exp2((score - top) * (SCALING * LOG2E))
                e_ref[n] = e
                dp_ref[n] = grad_prob
                stat_ref[n, 0:1] = top
                stat_ref[n, 1:2] = jnp.sum(folded(jnp.add, e), axis=0, keepdims=True)
                stat_ref[n, 2:3] = jnp.sum(folded(jnp.add, e * grad_prob), axis=0, keepdims=True)

        left = lax.broadcasted_iota(jnp.int32, (1, 2 * TILE), 1) < TILE
        tops = [
            stat_ref[n, 0:1] - jnp.where(left, mask_ref[a * POOL + slot], mask_ref[(a + 1) * POOL + slot])
            for n, (_, _, slot) in enumerate(slots)
        ]
        top = functools.reduce(jnp.maximum, tops)
        weights = [jnp.exp2((t - top) * (SCALING * LOG2E)) for t in tops]
        total = sum(w * stat_ref[n, 1:2] for n, w in enumerate(weights))
        delta = sum(w * stat_ref[n, 2:3] for n, w in enumerate(weights)) / total
        inverse = 1.0 / total
        for n, weight in enumerate(weights):
            stat_ref[n, 3:4] = weight * inverse

        out = jnp.zeros((HD, 2 * TILE), jnp.float32)
        dq = jnp.zeros((HD, 2 * TILE), jnp.float32)
        for f in range(FRAMES):
            values, keys = pairs(f)
            probs, grad_scores = [], []
            for u in range(count):
                n = f * count + u
                p = e_ref[n] * stat_ref[n, 3:4]
                probs.append(p.astype(jnp.bfloat16))
                grad_scores.append((p * (dp_ref[n] - delta)).astype(jnp.bfloat16))
            pb = jnp.concatenate(probs, axis=0)
            ds = jnp.concatenate(grad_scores, axis=0)
            dv = dot(pb, cotangents, nn)
            dk = dot(ds, queries, nn)
            for u in range(count):
                slot = f * TILES_DEV + start + u
                acc_ref[i, 0, slot] += dv[tile(u)]
                acc_ref[i, 1, slot] += dk[tile(u)]
            out = out + dot(values, pb, tn)
            dq = dq + dot(keys, ds, tn)
        o_ref[i, pl.ds(a, 2)] = out.T.astype(jnp.bfloat16).reshape(2, TILE, HD)
        dq_ref[i, pl.ds(a, 2)] = (dq.T * SCALING).astype(jnp.bfloat16).reshape(2, TILE, HD)

    barrier, greetings = greet_all(slab, head, devices, (above, below))
    for x in range(4):
        for i in range(heads):
            local(x, i).start()
    tables = [
        pltpu.make_async_copy(list_hbm, list_ref, table_sem.at[0]),
        pltpu.make_async_copy(count_hbm, count_ref, table_sem.at[1]),
    ]
    for table in tables:
        table.start()
    pl.semaphore_wait(barrier, greetings)
    send(0, (0,))
    send(0, (1,))
    for i in range(heads):
        forward_own(i)
    for i in range(1, heads):
        send(i, (0, 1))

    forward_halves()
    for i in range(heads):
        send(i, (2, 3))
    for i in range(1, heads):
        forward(i)

    for table in tables:
        table.wait()

    def masks(a, _):
        used = count_ref[slab * TILES_DEV + a]
        listed = [
            jnp.where(j < used, list_ref[j, slab * TILES_DEV + a] - (slab - 1) * TILES_DEV, -1)
            for j in range(LIST)
        ]

        def one(slot, _):
            hit = functools.reduce(jnp.logical_or, [entry == slot for entry in listed])
            mask_ref[a * POOL + slot] = jnp.where(hit, 0.0, UNUSED).astype(jnp.float32)
            return 0

        lax.fori_loop(0, POOL, one, 0)
        return 0

    lax.fori_loop(0, TILES_DEV, masks, 0)


    others = pl.ds(0, devices - 1)

    def leave(i):
        def parts(r, _):
            for side, (ref, (_, h)) in enumerate(((up_ref, above), (low_ref, below))):
                tile = lax.rem(h + 1 + r, devices)
                slot = 2 * TILES_DEV * (1 - side) + tile
                for kind in range(2):
                    ref[i, tile, kind] = acc_ref[i, kind, slot].astype(jnp.bfloat16)
                part(i, side, tile).start()
            return 0

        lax.fori_loop(0, devices, parts, 0)

        def both(peer):
            result(0, i, peer).start()
            result(1, i, peer).start()

        peers(both)
        result_local(0, i).start()
        result_local(1, i).start()

    def head_step(i, _):
        @pl.when(i > 0)
        def _():
            leave(i - 1)

        def clear(slot, _):
            for kind in range(2):
                acc_ref[i, kind, slot] = jnp.zeros((TILE, HD), jnp.float32)
            return 0

        lax.fori_loop(0, POOL, clear, 0)

        for x in (2, 3):
            local(x, i).wait()
            whole(q_ref.at[i, others], in_send.at[i, x], qg_recv.at[i, x - 2]).wait_recv()
        for side in range(2):
            whole(
                kv_ref.at[i, pl.ds(TILES_DEV, TILES_DEV)], rim_send.at[i, side], rim_recv.at[i, side]
            ).wait_recv()

        def first_finish(r):
            @pl.when(i == heads - 1)
            def _():
                finish(0, lax.rem(r + 1, devices))
                finish(0, lax.rem(r + 2, devices))

        def outer(n, _):
            attend(i, 6 * n, 4 * n, 4)
            first_finish(2 * n)
            return 0

        def inner(n, _):
            attend(i, 2 * n + 2, 2 * n, 6)
            first_finish(2 * n + 4)
            return 0

        lax.fori_loop(0, 2, outer, 0)
        lax.fori_loop(0, 2, inner, 0)
        return 0

    lax.fori_loop(0, heads, head_step, 0)
    leave(heads - 1)

    def settle_arrivals(i, _):
        for x in range(4):
            whole(q_ref.at[i, others], in_send.at[i, x], out_recv.at[i, x]).wait_send()
        for side in range(2):
            whole(
                kv_ref.at[i, pl.ds(TILES_DEV, TILES_DEV)], rim_send.at[i, side], rim_recv.at[i, side]
            ).wait_send()
        return 0

    lax.fori_loop(0, heads, settle_arrivals, 0)

    def last(n, _):
        finish(1 + lax.div(n, devices), lax.rem(n + 1, devices))
        return 0

    lax.fori_loop(0, (heads - 1) * devices, last, 0)

    def settle_results(i, _):
        for x in range(4):
            result_local(x, i).wait()
            whole(q_ref.at[i, others], out_send.at[i, x], out_recv.at[i, x]).wait()
        for side in range(2):
            whole(low_ref.at[i], part_send.at[i, side], part_recv.at[i, side, 0]).wait_send()
        return 0

    lax.fori_loop(0, heads, settle_results, 0)


def fused(tile_list, tile_count, key, value, query, cotangent):
    heads = key.shape[1] // (TILES_DEV * HD)
    hbm = pl.BlockSpec(memory_space=pl.ANY)
    tokens = jax.ShapeDtypeStruct(key.shape, jnp.bfloat16)
    tiles = pltpu.VMEM((heads, TILES_DEV, TILE, HD), jnp.bfloat16)
    pairs = pltpu.VMEM((heads, TILES_DEV, 2, TILE, HD), jnp.bfloat16)
    dma = pltpu.SemaphoreType.DMA
    return pl.pallas_call(
        functools.partial(fused_kernel, heads),
        out_shape=(pltpu.VMEM(key.shape, jnp.bfloat16),) * 4,
        in_specs=[hbm] * 6,
        out_specs=(hbm,) * 4,
        scratch_shapes=[
            pltpu.SMEM(tile_list.shape, jnp.int32),
            pltpu.SMEM(tile_count.shape, jnp.int32),
            dma((2,)),
            pltpu.VMEM((heads, POOL, 2, TILE, HD), jnp.bfloat16),
            tiles,
            tiles,
            pltpu.VMEM((heads, 2, POOL, TILE, HD), jnp.float32),
            pltpu.SMEM((TILES_DEV * POOL,), jnp.float32),
            pltpu.VMEM((6 * FRAMES, TILE, 2 * TILE), jnp.float32),
            pltpu.VMEM((6 * FRAMES, TILE, 2 * TILE), jnp.float32),
            pltpu.VMEM((6 * FRAMES, 8, 2 * TILE), jnp.float32),
            tiles,
            tiles,
            tiles,
            tiles,
            pairs,
            pairs,
            pairs,
            pairs,
            dma((heads, 4)),
            dma((heads, 2, TILES_DEV)),
            dma((heads, 2)),
            dma((heads, 4)),
            dma((heads, 2)),
            dma((heads, 2)),
            dma((heads, 4)),
            dma((heads, 4)),
            dma((heads, 4)),
            dma((heads, 2, TILES_DEV)),
            dma((heads, 2)),
        ],
        compiler_params=pltpu.CompilerParams(
            collective_id=0, has_side_effects=True, vmem_limit_bytes=36 * 2**20
        ),
        name="fused",
    )(tile_list, tile_count, key, value, query, cotangent)


def emit_kernel(*refs):
    count = len(refs) // 2
    sem = refs[-1]
    stores = [pltpu.make_async_copy(refs[n], refs[count + n], sem.at[n]) for n in range(count)]
    for store in stores:
        store.start()
    for store in stores:
        store.wait()


def emit(arrays):
    hbm = pl.BlockSpec(memory_space=pl.ANY)
    arrays = [pltpu.with_memory_space_constraint(a, pltpu.VMEM) for a in arrays]
    return pl.pallas_call(
        emit_kernel,
        out_shape=tuple(pltpu.HBM(a.shape, a.dtype) for a in arrays),
        in_specs=[hbm] * len(arrays),
        out_specs=(hbm,) * len(arrays),
        scratch_shapes=[pltpu.SemaphoreType.DMA((len(arrays),))],
        name="emit",
    )(*arrays)


def per_device(query, key, value, grad_out, tile_list, tile_count):
    tile_list, tile_count, query, key, value, grad_out = (
        pltpu.with_memory_space_constraint(x, pltpu.HBM)
        for x in (tile_list.T, tile_count, query, key, value, grad_out)
    )
    return tuple(emit(fused(tile_list, tile_count, key, value, query, grad_out)))


def solution(mesh):
    tokens = P(("seq", "head"), None)
    return jax.shard_map(
        per_device,
        mesh=mesh,
        in_specs=(tokens, tokens, tokens, tokens, P(), P()),
        out_specs=(tokens, tokens, tokens, tokens),
        check_vma=False,
    )
```
